32 devices in a mesh: tile: 16 (over z, x, core), mem: 2 (over y).
Axes of the slice: x: 2, y: 2, z: 4, core: 2. Of those that a mesh axis runs over, the one named last changes fastest.
Arguments:
- ensemble: float32 [64, 7, 32768], P('mem', None, 'tile'), may hold values from -6 to 6
- obs_site: int32 [8, 32], replicated, may hold values from 0 to 14335
- obs_value: float32 [8, 32], replicated, may hold values from -8 to 8
- obs_var: float32 [8, 32], replicated, may hold values from 4 to 32
- owner_tile: int32 [8], replicated, may hold values from 0 to 15
- tile_mask: int32 [8, 16], replicated, may hold values 0 or 1
- batch_order: int32 [8], replicated, may hold values from 0 to 7, each once
Outputs:
- posterior: float32 [64, 7, 32768], P('mem', None, 'tile')
The draws below stay inside these ranges and needn't reach their ends.
All inputs are finite; a program needn't handle non-finite values.
Results may differ from the reference program's by a relative error of at most 0.0001.
Values sent between devices are 32-bit elements; how exact they have to be, the bound alone decides.
No kernel may reach another device: no remote copies, remote signals or barrier semaphores. Data moves between devices by JAX's collectives and lax.ppermute only.
A program may use at most 64 MiB of HBM per device.

```python
import math
import jax
import jax.numpy as jnp
from jax import lax

MEMBERS = 64
CHANNELS = 7
CELL_DEV = 2048
BATCHES = 8
OBS_BATCH = 32
CELLS = 32768
N_TILE = 16


def set_ends(drawn, key, low, largest):
    longest = drawn.shape.index(max(drawn.shape))
    spots = []
    for shift in (0, 1):
        where = [jax.random.randint(jax.random.fold_in(key, axis), (), 0, length) for axis, length in enumerate(drawn.shape)]
        where[longest] = (where[longest] + shift) % drawn.shape[longest]
        spots.append(tuple(where))
    return drawn.at[spots[0]].set(low).at[spots[1]].set(largest)


def shard_levels(own_key, extent, split, least, top_value):
    def one(dim, shards_of):
        draws = jax.random.uniform(jax.random.fold_in(jax.random.fold_in(own_key, 6), dim), (shards_of,), jnp.float32, least / len(split), top_value / len(split))
        return jnp.repeat(jnp.exp(draws), extent[dim] // shards_of).reshape((-1,) + (1,) * (len(extent) - dim - 1))

    gain = one(*split[0])
    for cut in split[1:]:
        gain = gain * one(*cut)
    return gain


def scatter_about(stream_key, shape, scale, limit, shards=(), kind=jnp.bfloat16):
    array = jax.random.normal(stream_key, shape, jnp.float32) * scale
    if len(shards) > 0:
        array = shard_levels(stream_key, shape, shards, -0.22, 0.18) * array
    return jnp.clip(array, min=-limit, max=limit).astype(kind)


def setup_inputs(seed: int = 0) -> dict:
    arg_keys = jax.random.split(jax.random.key(seed), 8)
    return {
        "ensemble": scatter_about(arg_keys[0], (MEMBERS, CHANNELS, CELLS), 1.0, 6.0, ((0, 2), (2, 16)), jnp.float32),
        "obs_site": set_ends(jax.random.randint(arg_keys[1], (BATCHES, OBS_BATCH), 0, CHANNELS * CELL_DEV), jax.random.fold_in(arg_keys[1], 1), 0, (CHANNELS * CELL_DEV) - 1).astype(jnp.int32),
        "obs_value": scatter_about(arg_keys[2], (BATCHES, OBS_BATCH), 1.5, 8.0, (), jnp.float32),
        "obs_var": jnp.clip(jnp.exp(jax.random.uniform(arg_keys[3], (BATCHES, OBS_BATCH), jnp.float32, math.log(4.0), math.log(32.0))), 4.0, 32.0),
        "owner_tile": set_ends(jax.random.randint(arg_keys[4], (BATCHES,), 0, N_TILE), jax.random.fold_in(arg_keys[4], 1), 0, N_TILE - 1).astype(jnp.int32),
        "tile_mask": set_ends((jax.random.randint(arg_keys[5], (BATCHES, N_TILE), 0, 2) < 1).astype(jnp.int32), jax.random.fold_in(arg_keys[5], 1), 0, 1),
        "batch_order": jax.random.permutation(arg_keys[6], BATCHES).astype(jnp.int32),
    }


def batch_transform(priors, values, variances):
    count = priors.shape[1]
    highest = lax.Precision.HIGHEST

    def assimilate(transform, inputs):
        prior_row, value, variance = inputs
        y_row = jnp.dot(prior_row, transform, precision=highest)
        ens_mean = jnp.mean(y_row)
        spread = y_row - ens_mean
        sample_var = jnp.sum(spread * spread) / (count - 1)
        inv_total = 1.0 / (sample_var + variance)
        alpha = 1.0 / (1.0 + jnp.sqrt(variance * inv_total))
        weights = inv_total / (count - 1) * (value - ens_mean - alpha * spread)
        moved = jnp.dot(transform, spread, precision=highest)
        return (transform + moved[:, None] * weights[None, :], None)
    start_eye = jnp.eye(count, dtype=jnp.float32)
    result, _ = lax.scan(assimilate, start_eye, (priors, values, variances))
    return result

def reference(ensemble, obs_site, obs_value, obs_var, owner_tile, tile_mask, batch_order):
    highest = lax.Precision.HIGHEST
    count = ensemble.shape[0]
    state_four = ensemble.reshape(count, CHANNELS, N_TILE, CELL_DEV)
    state_grid = state_four.transpose(0, 2, 1, 3).reshape(count, N_TILE, CHANNELS * CELL_DEV)
    tile_ids = jnp.arange(N_TILE, dtype=jnp.int32)
    combined = jnp.broadcast_to(jnp.eye(count, dtype=jnp.float32), (N_TILE, count, count))
    for position in range(BATCHES):
        batch_id = batch_order[position]
        owner = owner_tile[batch_id]
        owner_rows = jnp.take(state_grid, owner, axis=1)
        obs_rows = jnp.take(owner_rows, obs_site[batch_id], axis=1)
        priors = jnp.dot(obs_rows.T, combined[owner], precision=highest)
        transform = batch_transform(priors, obs_value[batch_id], obs_var[batch_id])
        is_active = (tile_mask[batch_id] == 1) | (tile_ids == owner)
        updated = jnp.einsum('tij,jk->tik', combined, transform, precision=highest)
        combined = jnp.where(is_active[:, None, None], updated, combined)

    def apply_tile(inputs):
        matrix, block = inputs
        return jnp.einsum('mn,mvc->nvc', matrix, block, precision=highest)
    per_tile = lax.map(apply_tile, (combined, state_four.transpose(2, 0, 1, 3)))
    return per_tile.transpose(1, 2, 0, 3).reshape(count, CHANNELS, N_TILE * CELL_DEV)
```

```python
import functools

import jax
import jax.numpy as jnp
from jax import lax
from jax.experimental import pallas as pl
from jax.experimental.pallas import tpu as pltpu
from jax.sharding import PartitionSpec as P

LANES = 128
SUBS = 8
SMEM = pl.BlockSpec(memory_space=pltpu.SMEM)
VMEM = pl.BlockSpec(memory_space=pltpu.VMEM)


def gather_kernel(site_ref, owner_ref, order_ref, tile_ref, ens_ref, out_ref):
    batches, obs = site_ref.shape
    cells = ens_ref.shape[2]
    members = ens_ref.shape[1]
    per = LANES // obs
    lane = lax.broadcasted_iota(jnp.int32, (members, LANES), 1)
    out_ref[...] = jnp.zeros_like(out_ref)

    def one(p, carry):
        b = order_ref[p]

        @pl.when(owner_ref[b] == tile_ref[0])
        def _():
            base = lax.rem(p, per) * obs
            spot = pl.ds(pl.multiple_of(lax.div(p, per) * LANES, LANES), LANES)
            acc = out_ref[:, spot]
            for k in range(obs):
                site = site_ref[b, k]
                chan = lax.div(site, cells)
                cell = site - chan * cells
                col = lax.rem(cell, LANES)
                start = pl.multiple_of(cell - col, LANES)
                block = ens_ref[chan, :, pl.ds(start, LANES)]
                at = base + k
                turned = pltpu.roll(block, lax.rem(at - col + LANES, LANES), 1)
                acc = jnp.where(lane == at, turned, acc)
            out_ref[:, spot] = acc

        return carry

    lax.fori_loop(0, batches, one, 0)


def gather_rows(ens, obs_site, owner_tile, batch_order, tile):
    batches, obs = obs_site.shape
    return pl.pallas_call(
        gather_kernel,
        out_shape=jax.ShapeDtypeStruct((ens.shape[1], batches * obs), jnp.float32),
        in_specs=[SMEM, SMEM, SMEM, SMEM, VMEM],
        out_specs=VMEM,
        name="gather_rows",
    )(obs_site, owner_tile, batch_order, tile, ens)


def spread(row):
    return jnp.broadcast_to(row, (SUBS, row.shape[1]))


def chain_kernel(order_ref, owner_ref, mask_ref, var_ref, tile_ref, own_ref, oth_ref, val_ref,
                 out_ref, w_ref, left_ref, right_ref, z_ref, v_ref, val_s):
    batches, obs = val_ref.shape
    half = own_ref.shape[0]
    members = 2 * half
    total = batches * obs
    tiles = total // LANES
    per = LANES // obs
    blocks = obs // SUBS
    width = w_ref.shape[0]
    inv = 1.0 / (members - 1)
    highest = lax.Precision.HIGHEST
    contract = functools.partial(
        lax.dot_general, dimension_numbers=(((0,), (0,)), ((), ())), precision=highest,
        preferred_element_type=jnp.float32)
    lane1 = lax.broadcasted_iota(jnp.int32, (1, LANES), 1)
    lane8 = lax.broadcasted_iota(jnp.int32, (SUBS, LANES), 1)
    sub8 = lax.broadcasted_iota(jnp.int32, (SUBS, LANES), 0)
    tile = tile_ref[0]

    val_s[...] = jnp.zeros_like(val_s)
    val_s[:, :obs] = val_ref[...]
    values = []
    for t in range(tiles):
        row = jnp.zeros((1, LANES), jnp.float32)
        for q in range(per):
            one = val_s[pl.ds(order_ref[t * per + q], 1), :]
            row = row + (pltpu.roll(one, q * obs, 1) if q else one)
        values.append(row)
    values = jnp.concatenate(values, axis=1)

    raw = jnp.concatenate([own_ref[...], oth_ref[...]], axis=0)
    mean = jnp.sum(raw, axis=0, keepdims=True) * (1.0 / members)
    anom = raw - mean
    first = lax.broadcasted_iota(jnp.int32, (SUBS, total), 0) == 0
    lhs = jnp.concatenate([anom, jnp.where(first, values - mean, 0.0)], axis=0)
    depth = members + SUBS
    r_i = lax.broadcasted_iota(jnp.int32, (depth, 2 * LANES), 0)
    l_i = lax.broadcasted_iota(jnp.int32, (depth, 2 * LANES), 1)
    pick = jnp.where((r_i < members) & ((l_i == r_i) | (l_i == r_i + members)), 1.0, 0.0)
    pick = jnp.where((r_i == members) & (l_i == LANES), 1.0, pick)
    rhs = jnp.concatenate(
        [jnp.concatenate([anom, jnp.zeros((SUBS, total), jnp.float32)], axis=0), pick], axis=1)
    full = contract(lhs, rhs)
    for t in range(width):
        w_ref[t] = full[:, t * LANES:(t + 1) * LANES]

    def batch(p, carry):
        b = order_ref[p]
        o = owner_ref[b]
        mine = (mask_ref[b, tile] == 1) | (o == tile)
        mine_f = jnp.where(mine, 1.0, 0.0)
        act = []
        late = []
        for t in range(tiles):
            row = jnp.zeros((1, LANES), jnp.float32)
            row_late = jnp.zeros((1, LANES), jnp.float32)
            for q in range(per):
                other = owner_ref[order_ref[t * per + q]]
                on = (mask_ref[b, other] == 1) | (o == other)
                here = (lane1 >= q * obs) & (lane1 < (q + 1) * obs)
                row = jnp.where(here, jnp.where(on, 1.0, 0.0), row)
                row_late = jnp.where(here, jnp.where(t * per + q > p, 1.0, 0.0), row_late)
            act.append(row)
            late.append(row_late)
        act8 = [spread(a) > 0.5 for a in act]
        z_on = jnp.where(lane8 < members, mine_f, 0.0) > 0.5
        pick_w = act8 + [z_on, lane8 == 0]
        pick_b = act8 + [z_on, lane8 < 0]

        start = pl.multiple_of(p * obs, obs)
        rows = pl.ds(start, obs)
        wp = [[w_ref[t, pl.ds(pl.multiple_of(start + i * SUBS, SUBS), SUBS), :] for i in range(blocks)]
              for t in range(width)]
        shift = lax.rem(LANES - lax.rem(p, per) * obs, LANES)
        gram = w_ref[lax.div(p, per), rows, :]
        gram = pltpu.roll(gram, shift, 1)
        cols = [[jnp.broadcast_to(gram[i * SUBS:(i + 1) * SUBS, j:j + 1], (SUBS, LANES)) if i >= j // SUBS else None
                 for i in range(blocks)] for j in range(obs)]
        for k in range(obs):
            kb, ks = k // SUBS, k % SUBS
            col = cols[k]
            var = var_ref[b, k]
            pivot = spread(col[kb][ks:ks + 1, :])
            g = 1.0 / (pivot * inv + var)
            weight = g * inv
            beta = weight / (1.0 + jnp.sqrt(var * g))
            below = [None] * blocks
            below[kb] = jnp.where(sub8 > ks, col[kb], 0.0)
            for i in range(kb + 1, blocks):
                below[i] = col[i]
            for j in range(k + 1, obs):
                jb, js = j // SUBS, j % SUBS
                factor = weight * spread(col[jb][js:js + 1, :])
                for i in range(jb, blocks):
                    cols[j][i] = cols[j][i] - col[i] * factor
            for t in range(width):
                wk = spread(wp[t][kb][ks:ks + 1, :])
                both = jnp.where(pick_w[t], weight, beta) * wk
                single = jnp.where(pick_b[t], beta, 0.0) * wk
                right_ref[k:k + 1, t * LANES:(t + 1) * LANES] = both[:1]
                right_ref[obs + k:obs + k + 1, t * LANES:(t + 1) * LANES] = single[:1]
                for i in range(kb, blocks):
                    wp[t][i] = wp[t][i] - below[i] * both
        for t in range(tiles):
            for i in range(blocks):
                d = wp[t][i] * late[t]
                left_ref[i * SUBS:(i + 1) * SUBS, t * LANES:(t + 1) * LANES] = d * act[t]
                left_ref[obs + i * SUBS:obs + (i + 1) * SUBS, t * LANES:(t + 1) * LANES] = d * (1.0 - act[t])
        for i in range(blocks):
            at = pl.ds(pl.multiple_of(start + i * SUBS, SUBS), SUBS)
            z_ref[at, :] = wp[tiles][i] * mine_f
        gain = jnp.broadcast_to(right_ref[:obs, (width - 1) * LANES:(width - 1) * LANES + 1], (obs, LANES))
        v_ref[rows, :] = gain - right_ref[:obs, tiles * LANES:(tiles + 1) * LANES]

        @pl.when(p < batches - 1)
        def _():
            update = contract(left_ref[...], right_ref[...])
            for t in range(width):
                w_ref[t] = w_ref[t] - update[:, t * LANES:(t + 1) * LANES]

        return carry

    lax.fori_loop(0, batches, batch, 0)
    moved = contract(v_ref[...], z_ref[...])
    out_ref[...] = moved[members:members + half, :members]


def chain(own, oth, obs_value, obs_var, owner_tile, tile_mask, batch_order, tile):
    half, total = own.shape
    obs = obs_value.shape[1]
    width = total // LANES + 2
    f32 = jnp.float32
    return pl.pallas_call(
        chain_kernel,
        out_shape=jax.ShapeDtypeStruct((half, 2 * half), f32),
        in_specs=[SMEM] * 5 + [VMEM] * 3,
        out_specs=VMEM,
        scratch_shapes=[
            pltpu.VMEM((width, total, LANES), f32),
            pltpu.VMEM((2 * obs, total), f32),
            pltpu.VMEM((2 * obs, width * LANES), f32),
            pltpu.VMEM((total, LANES), f32),
            pltpu.VMEM((total, LANES), f32),
            pltpu.VMEM((obs_value.shape[0], LANES), f32),
        ],
        name="chain",
    )(batch_order, owner_tile, tile_mask, obs_var, tile, own, oth, obs_value)


def apply_kernel(mat_ref, own_ref, oth_ref, out_ref):
    half = mat_ref.shape[0]
    mat = mat_ref[...]
    high = mat.astype(jnp.bfloat16)
    low = (mat - high.astype(jnp.float32)).astype(jnp.bfloat16)
    left = jnp.concatenate(
        [jnp.concatenate([high, high], axis=1), jnp.concatenate([low, jnp.zeros_like(low)], axis=1)], axis=0)
    own = own_ref[0]
    x = jnp.concatenate([own, oth_ref[0]], axis=0)
    x_high = x.astype(jnp.bfloat16)
    x_low = (x - x_high.astype(jnp.float32)).astype(jnp.bfloat16)
    y = jnp.dot(left, jnp.concatenate([x_high, x_low], axis=0), preferred_element_type=jnp.float32)
    out_ref[0] = own + (y[:half] + y[half:])


def apply_matrix(mat, own, oth):
    chans, half, cells = own.shape
    spec = pl.BlockSpec((1, half, cells), lambda c: (c, 0, 0))
    return pl.pallas_call(
        apply_kernel,
        grid=(chans,),
        out_shape=jax.ShapeDtypeStruct(own.shape, jnp.float32),
        in_specs=[pl.BlockSpec(mat.shape, lambda c: (0, 0)), spec, spec],
        out_specs=spec,
        name="apply",
    )(mat, own, oth)


def body(ensemble, obs_site, obs_value, obs_var, owner_tile, tile_mask, batch_order):
    tile = lax.axis_index("tile").astype(jnp.int32).reshape(1)
    n_tile = lax.axis_size("tile")
    swap = [(0, 1), (1, 0)]
    ens = jnp.transpose(ensemble, (1, 0, 2))
    own = gather_rows(ens, obs_site, owner_tile, batch_order, tile)
    oth = lax.ppermute(own, "mem", swap)
    held, _ = lax.optimization_barrier((ens, own))
    bulk = lax.ppermute(held, "mem", swap)
    rows = jnp.concatenate([own, oth], axis=0)
    step = 1
    while step < n_tile:
        rows = rows + lax.ppermute(rows, "tile", [(i, i ^ step) for i in range(n_tile)])
        step *= 2
    half = own.shape[0]
    mat = chain(rows[:half], rows[half:], obs_value, obs_var, owner_tile, tile_mask, batch_order, tile)
    out = apply_matrix(mat, ens, bulk)
    return jnp.transpose(out, (1, 0, 2))


def solution(mesh):
    return jax.shard_map(
        body,
        mesh=mesh,
        in_specs=(P("mem", None, "tile"), P(), P(), P(), P(), P(), P()),
        out_specs=P("mem", None, "tile"),
        check_vma=False,
    )
```

```python
import functools

import jax
import jax.numpy as jnp
from jax import lax
from jax.experimental import pallas as pl
from jax.experimental.pallas import tpu as pltpu
from jax.sharding import PartitionSpec as P


LANES = 128
SUBS = 8
SMEM = pl.BlockSpec(memory_space=pltpu.SMEM)
VMEM = pl.BlockSpec(memory_space=pltpu.VMEM)


def gather_kernel(site_ref, owner_ref, order_ref, tile_ref, ens_ref, out_ref):
    batches, obs = site_ref.shape
    cells = ens_ref.shape[2]
    members = ens_ref.shape[1]
    per = LANES // obs
    lane = lax.broadcasted_iota(jnp.int32, (members, LANES), 1)
    out_ref[...] = jnp.zeros_like(out_ref)

    def one(p, carry):
        b = order_ref[p]

        @pl.when(owner_ref[b] == tile_ref[0])
        def _():
            base = lax.rem(p, per) * obs
            spot = pl.ds(pl.multiple_of(lax.div(p, per) * LANES, LANES), LANES)
            acc = out_ref[:, spot]
            for k in range(obs):
                site = site_ref[b, k]
                chan = lax.div(site, cells)
                cell = site - chan * cells
                col = lax.rem(cell, LANES)
                start = pl.multiple_of(cell - col, LANES)
                block = ens_ref[chan, :, pl.ds(start, LANES)]
                at = base + k
                turned = pltpu.roll(block, lax.rem(at - col + LANES, LANES), 1)
                acc = jnp.where(lane == at, turned, acc)
            out_ref[:, spot] = acc

        return carry

    lax.fori_loop(0, batches, one, 0)


def gather_rows(ens, obs_site, owner_tile, batch_order, tile):
    batches, obs = obs_site.shape
    return pl.pallas_call(
        gather_kernel,
        out_shape=jax.ShapeDtypeStruct((ens.shape[1], batches * obs), jnp.float32),
        in_specs=[SMEM, SMEM, SMEM, SMEM, VMEM],
        out_specs=VMEM,
        compiler_params=pltpu.CompilerParams(vmem_limit_bytes=4 << 20),
        name="gather_rows",
    )(obs_site, owner_tile, batch_order, tile, ens)


def spread(row):
    return jnp.broadcast_to(row, (SUBS, row.shape[1]))


def chain_kernel(order_ref, owner_ref, mask_ref, var_ref, tile_ref, raw_ref, val_ref,
                 out_ref, w_ref, left_ref, right_ref, z_ref, v_ref, val_s):
    batches, obs = val_ref.shape
    members = raw_ref.shape[0]
    half = members // 2
    total = batches * obs
    tiles = total // LANES
    per = LANES // obs
    blocks = obs // SUBS
    width = w_ref.shape[0]
    inv = 1.0 / (members - 1)
    highest = lax.Precision.HIGHEST
    contract = functools.partial(
        lax.dot_general, dimension_numbers=(((0,), (0,)), ((), ())), precision=highest,
        preferred_element_type=jnp.float32)
    lane1 = lax.broadcasted_iota(jnp.int32, (1, LANES), 1)
    lane8 = lax.broadcasted_iota(jnp.int32, (SUBS, LANES), 1)
    sub8 = lax.broadcasted_iota(jnp.int32, (SUBS, LANES), 0)
    tile = tile_ref[0]

    val_s[...] = jnp.zeros_like(val_s)
    val_s[:, :obs] = val_ref[...]
    values = []
    for t in range(tiles):
        row = jnp.zeros((1, LANES), jnp.float32)
        for q in range(per):
            one = val_s[pl.ds(order_ref[t * per + q], 1), :]
            row = row + (pltpu.roll(one, q * obs, 1) if q else one)
        values.append(row)
    values = jnp.concatenate(values, axis=1)

    raw = raw_ref[...]
    mean = jnp.sum(raw, axis=0, keepdims=True) * (1.0 / members)
    anom = raw - mean
    first = lax.broadcasted_iota(jnp.int32, (SUBS, total), 0) == 0
    lhs = jnp.concatenate([anom, jnp.where(first, values - mean, 0.0)], axis=0)
    depth = members + SUBS
    r_i = lax.broadcasted_iota(jnp.int32, (depth, 2 * LANES), 0)
    l_i = lax.broadcasted_iota(jnp.int32, (depth, 2 * LANES), 1)
    pick = jnp.where((r_i < members) & ((l_i == r_i) | (l_i == r_i + members)), 1.0, 0.0)
    pick = jnp.where((r_i == members) & (l_i == LANES), 1.0, pick)
    rhs = jnp.concatenate(
        [jnp.concatenate([anom, jnp.zeros((SUBS, total), jnp.float32)], axis=0), pick], axis=1)
    full = contract(lhs, rhs)
    for t in range(width):
        w_ref[t] = full[:, t * LANES:(t + 1) * LANES]

    def batch(p, carry):
        b = order_ref[p]
        o = owner_ref[b]
        mine = (mask_ref[b, tile] == 1) | (o == tile)
        mine_f = jnp.where(mine, 1.0, 0.0)
        act = []
        late = []
        for t in range(tiles):
            row = jnp.zeros((1, LANES), jnp.float32)
            row_late = jnp.zeros((1, LANES), jnp.float32)
            for q in range(per):
                other = owner_ref[order_ref[t * per + q]]
                on = (mask_ref[b, other] == 1) | (o == other)
                here = (lane1 >= q * obs) & (lane1 < (q + 1) * obs)
                row = jnp.where(here, jnp.where(on, 1.0, 0.0), row)
                row_late = jnp.where(here, jnp.where(t * per + q > p, 1.0, 0.0), row_late)
            act.append(row)
            late.append(row_late)
        act8 = [spread(a) > 0.5 for a in act]
        z_on = jnp.where(lane8 < members, mine_f, 0.0) > 0.5
        pick_w = act8 + [z_on, lane8 == 0]
        pick_b = act8 + [z_on, lane8 < 0]

        start = pl.multiple_of(p * obs, obs)
        rows = pl.ds(start, obs)
        wp = [[w_ref[t, pl.ds(pl.multiple_of(start + i * SUBS, SUBS), SUBS), :] for i in range(blocks)]
              for t in range(width)]
        shift = lax.rem(LANES - lax.rem(p, per) * obs, LANES)
        gram = w_ref[lax.div(p, per), rows, :]
        gram = pltpu.roll(gram, shift, 1)
        cols = [[jnp.broadcast_to(gram[i * SUBS:(i + 1) * SUBS, j:j + 1], (SUBS, LANES)) if i >= j // SUBS else None
                 for i in range(blocks)] for j in range(obs)]
        for k in range(obs):
            kb, ks = k // SUBS, k % SUBS
            col = cols[k]
            var = var_ref[b, k]
            pivot = spread(col[kb][ks:ks + 1, :])
            g = 1.0 / (pivot * inv + var)
            weight = g * inv
            beta = weight / (1.0 + jnp.sqrt(var * g))
            below = [None] * blocks
            below[kb] = jnp.where(sub8 > ks, col[kb], 0.0)
            for i in range(kb + 1, blocks):
                below[i] = col[i]
            for j in range(k + 1, obs):
                jb, js = j // SUBS, j % SUBS
                factor = weight * spread(col[jb][js:js + 1, :])
                for i in range(jb, blocks):
                    cols[j][i] = cols[j][i] - col[i] * factor
            for t in range(width):
                wk = spread(wp[t][kb][ks:ks + 1, :])
                both = jnp.where(pick_w[t], weight, beta) * wk
                single = jnp.where(pick_b[t], beta, 0.0) * wk
                right_ref[k:k + 1, t * LANES:(t + 1) * LANES] = both[:1]
                right_ref[obs + k:obs + k + 1, t * LANES:(t + 1) * LANES] = single[:1]
                for i in range(kb, blocks):
                    wp[t][i] = wp[t][i] - below[i] * both
        for t in range(tiles):
            for i in range(blocks):
                d = wp[t][i] * late[t]
                left_ref[i * SUBS:(i + 1) * SUBS, t * LANES:(t + 1) * LANES] = d * act[t]
                left_ref[obs + i * SUBS:obs + (i + 1) * SUBS, t * LANES:(t + 1) * LANES] = d * (1.0 - act[t])
        for i in range(blocks):
            at = pl.ds(pl.multiple_of(start + i * SUBS, SUBS), SUBS)
            z_ref[at, :] = wp[tiles][i] * mine_f
        gain = jnp.broadcast_to(right_ref[:obs, (width - 1) * LANES:(width - 1) * LANES + 1], (obs, LANES))
        v_ref[rows, :] = gain - right_ref[:obs, tiles * LANES:(tiles + 1) * LANES]

        @pl.when(p < batches - 1)
        def _():
            update = contract(left_ref[...], right_ref[...])
            for t in range(width):
                w_ref[t] = w_ref[t] - update[:, t * LANES:(t + 1) * LANES]

        return carry

    lax.fori_loop(0, batches, batch, 0)
    moved = contract(v_ref[...], z_ref[...])
    out_ref[...] = moved[members:members + half, :members]


def chain(rows, obs_value, obs_var, owner_tile, tile_mask, batch_order, tile):
    members, total = rows.shape
    half = members // 2
    obs = obs_value.shape[1]
    width = total // LANES + 2
    f32 = jnp.float32
    return pl.pallas_call(
        chain_kernel,
        out_shape=jax.ShapeDtypeStruct((half, members), f32),
        in_specs=[SMEM] * 5 + [VMEM] * 2,
        out_specs=VMEM,
        scratch_shapes=[
            pltpu.VMEM((width, total, LANES), f32),
            pltpu.VMEM((2 * obs, total), f32),
            pltpu.VMEM((2 * obs, width * LANES), f32),
            pltpu.VMEM((total, LANES), f32),
            pltpu.VMEM((total, LANES), f32),
            pltpu.VMEM((obs_value.shape[0], LANES), f32),
        ],
        compiler_params=pltpu.CompilerParams(vmem_limit_bytes=8 << 20),
        name="chain",
    )(batch_order, owner_tile, tile_mask, obs_var, tile, rows, obs_value)


def apply_kernel(mat_ref, own_ref, *rest):
    oth_refs, out_ref = rest[:-1], rest[-1]
    half = mat_ref.shape[0]
    oth = oth_refs[0][0]
    mat = mat_ref[...]
    high = mat.astype(jnp.bfloat16)
    low = (mat - high.astype(jnp.float32)).astype(jnp.bfloat16)
    left = jnp.concatenate(
        [jnp.concatenate([high, high], axis=1), jnp.concatenate([low, jnp.zeros_like(low)], axis=1)], axis=0)
    own = own_ref[0]
    x = jnp.concatenate([own, oth], axis=0)
    x_high = x.astype(jnp.bfloat16)
    x_low = (x - x_high.astype(jnp.float32)).astype(jnp.bfloat16)
    y = jnp.dot(left, jnp.concatenate([x_high, x_low], axis=0), preferred_element_type=jnp.float32)
    out_ref[0] = own + (y[:half] + y[half:])


def apply_first(mat_ref, own_ref, oth_ref, out_ref):
    apply_kernel(mat_ref, own_ref, oth_ref, out_ref)


def apply_next(mat_ref, own_ref, oth_ref, prev_ref, out_ref):
    apply_kernel(mat_ref, own_ref, oth_ref, out_ref)


def apply_matrix(mat, own, oth, start, out):
    _, half, cells = own.shape
    here = oth.shape[0]
    spec = pl.BlockSpec((1, half, cells), lambda c: (c, 0, 0))
    shifted = pl.BlockSpec((1, half, cells), lambda c: (c + start, 0, 0))
    args = [mat, own, oth]
    in_specs = [pl.BlockSpec(mat.shape, lambda c: (0, 0)), shifted, spec]
    alias = {}
    if out is not None:
        args.append(out)
        in_specs.append(pl.BlockSpec(memory_space=pl.ANY))
        alias = {3: 0}
    return pl.pallas_call(
        apply_first if out is None else apply_next,
        grid=(here,),
        out_shape=jax.ShapeDtypeStruct(own.shape, jnp.float32),
        in_specs=in_specs,
        out_specs=shifted,
        input_output_aliases=alias,
        compiler_params=pltpu.CompilerParams(vmem_limit_bytes=8 << 20),
        name="apply",
    )(*args)


def body(ensemble, obs_site, obs_value, obs_var, owner_tile, tile_mask, batch_order):
    tile = lax.axis_index("tile").astype(jnp.int32).reshape(1)
    n_tile = lax.axis_size("tile")
    swap = [(0, 1), (1, 0)]
    ens = jnp.transpose(ensemble, (1, 0, 2))
    chans = ens.shape[0]
    first = lax.ppermute(ens[:1], "mem", swap)
    own = gather_rows(ens, obs_site, owner_tile, batch_order, tile)
    oth = lax.ppermute(own, "mem", swap)
    mid = lax.ppermute(ens[1:chans - 1], "mem", swap)
    last = lax.ppermute(ens[chans - 1:], "mem", swap)
    rows = jnp.concatenate([own, oth], axis=0)
    step = 1
    while step < n_tile:
        rows = rows + lax.ppermute(rows, "tile", [(i, i ^ step) for i in range(n_tile)])
        step *= 2
    mat = chain(rows, obs_value, obs_var, owner_tile, tile_mask, batch_order, tile)
    out = apply_matrix(mat, ens, first, 0, None)
    out = apply_matrix(mat, ens, mid, 1, out)
    out = apply_matrix(mat, ens, last, chans - 1, out)
    return jnp.transpose(out, (1, 0, 2))


def solution(mesh):
    return jax.shard_map(
        body,
        mesh=mesh,
        in_specs=(P("mem", None, "tile"), P(), P(), P(), P(), P(), P()),
        out_specs=P("mem", None, "tile"),
        check_vma=False,
    )
```

```python
import functools

import jax
import jax.numpy as jnp
from jax import lax
from jax.experimental import pallas as pl
from jax.experimental.pallas import tpu as pltpu
from jax.sharding import PartitionSpec as P


LANES = 128
SUBS = 8
SMEM = pl.BlockSpec(memory_space=pltpu.SMEM)
VMEM = pl.BlockSpec(memory_space=pltpu.VMEM)
ANY = pl.BlockSpec(memory_space=pl.ANY)


def hbm(x):
    return pltpu.with_memory_space_constraint(x, pltpu.HBM)


def vmem(x):
    return pltpu.with_memory_space_constraint(x, pltpu.VMEM)


def first_kernel(units_hbm, first_ref, sem):
    copy = pltpu.make_async_copy(units_hbm.at[pl.ds(0, first_ref.shape[0])], first_ref, sem)
    copy.start()
    copy.wait()


def first_units(units, count):
    return pl.pallas_call(
        first_kernel,
        out_shape=pltpu.VMEM((count,) + units.shape[1:], jnp.float32),
        in_specs=[ANY],
        out_specs=VMEM,
        scratch_shapes=[pltpu.SemaphoreType.DMA],
        name="first_units",
    )(hbm(units))


def gather_kernel(site_hbm, owner_hbm, order_hbm, units_hbm, rows_ref, main_hbm, last_ref,
                  held_ref, site_ref, owner_ref, order_ref, sem):
    batches, obs = site_hbm.shape
    count, half, cells = units_hbm.shape
    per = LANES // obs
    tail = last_ref.shape[0]
    middle = main_hbm.shape[0]
    state = pltpu.make_async_copy(units_hbm, held_ref, sem.at[0])
    small = [
        pltpu.make_async_copy(site_hbm, site_ref, sem.at[1]),
        pltpu.make_async_copy(owner_hbm, owner_ref, sem.at[2]),
        pltpu.make_async_copy(order_hbm, order_ref, sem.at[3]),
    ]
    end = pltpu.make_async_copy(units_hbm.at[pl.ds(count - tail, tail)], last_ref, sem.at[4])
    for copy in small + [state, end]:
        copy.start()
    tile = lax.axis_index("tile")
    lane = lax.broadcasted_iota(jnp.int32, (half, LANES), 1)
    rows_ref[...] = jnp.zeros_like(rows_ref)
    state.wait()
    out = pltpu.make_async_copy(held_ref.at[pl.ds(count - tail - middle, middle)], main_hbm, sem.at[5])
    out.start()
    for copy in small:
        copy.wait()

    def one(p, carry):
        b = order_ref[p]

        @pl.when(owner_ref[b] == tile)
        def _():
            base = lax.rem(p, per) * obs
            spot = pl.ds(pl.multiple_of(lax.div(p, per) * LANES, LANES), LANES)
            acc = [rows_ref[h * half:(h + 1) * half, spot] for h in range(2)]
            for k in range(obs):
                site = site_ref[b, k]
                chan = lax.div(site, cells)
                cell = site - chan * cells
                col = lax.rem(cell, LANES)
                start = pl.multiple_of(cell - col, LANES)
                at = base + k
                turn = lax.rem(at - col + LANES, LANES)
                here = lane == at
                for h in range(2):
                    block = held_ref[2 * chan + h, :, pl.ds(start, LANES)]
                    acc[h] = jnp.where(here, pltpu.roll(block, turn, 1), acc[h])
            for h in range(2):
                rows_ref[h * half:(h + 1) * half, spot] = acc[h]

        return carry

    lax.fori_loop(0, batches, one, 0)
    end.wait()
    out.wait()


def gather_rows(units, obs_site, owner_tile, batch_order, head, tail):
    batches, obs = obs_site.shape
    count, half, cells = units.shape
    f32 = jnp.float32
    return pl.pallas_call(
        gather_kernel,
        out_shape=(
            pltpu.VMEM((2 * half, batches * obs), f32),
            pltpu.HBM((count - head - tail, half, cells), f32),
            pltpu.VMEM((tail, half, cells), f32),
        ),
        in_specs=[ANY] * 4,
        out_specs=(VMEM, ANY, VMEM),
        scratch_shapes=[
            pltpu.VMEM(units.shape, f32),
            pltpu.SMEM(obs_site.shape, jnp.int32),
            pltpu.SMEM(owner_tile.shape, jnp.int32),
            pltpu.SMEM(batch_order.shape, jnp.int32),
            pltpu.SemaphoreType.DMA((6,)),
        ],
        compiler_params=pltpu.CompilerParams(vmem_limit_bytes=8 << 20),
        name="gather_rows",
    )(hbm(obs_site), hbm(owner_tile), hbm(batch_order), hbm(units))


def spread(row):
    return jnp.broadcast_to(row, (SUBS, row.shape[1]))


def chain_kernel(order_ref, owner_ref, mask_ref, var_ref, tile_ref, raw_ref, val_ref,
                 out_ref, w_ref, left_ref, right_ref, z_ref, v_ref, val_s):
    batches, obs = val_ref.shape
    members = raw_ref.shape[0]
    half = members // 2
    total = batches * obs
    tiles = total // LANES
    per = LANES // obs
    blocks = obs // SUBS
    width = w_ref.shape[0]
    inv = 1.0 / (members - 1)
    highest = lax.Precision.HIGHEST
    contract = functools.partial(
        lax.dot_general, dimension_numbers=(((0,), (0,)), ((), ())), precision=highest,
        preferred_element_type=jnp.float32)
    lane1 = lax.broadcasted_iota(jnp.int32, (1, LANES), 1)
    lane8 = lax.broadcasted_iota(jnp.int32, (SUBS, LANES), 1)
    sub8 = lax.broadcasted_iota(jnp.int32, (SUBS, LANES), 0)
    tile = tile_ref[0]

    val_s[...] = jnp.zeros_like(val_s)
    val_s[:, :obs] = val_ref[...]
    values = []
    for t in range(tiles):
        row = jnp.zeros((1, LANES), jnp.float32)
        for q in range(per):
            one = val_s[pl.ds(order_ref[t * per + q], 1), :]
            row = row + (pltpu.roll(one, q * obs, 1) if q else one)
        values.append(row)
    values = jnp.concatenate(values, axis=1)

    raw = raw_ref[...]
    mean = jnp.sum(raw, axis=0, keepdims=True) * (1.0 / members)
    anom = raw - mean
    first = lax.broadcasted_iota(jnp.int32, (SUBS, total), 0) == 0
    lhs = jnp.concatenate([anom, jnp.where(first, values - mean, 0.0)], axis=0)
    depth = members + SUBS
    r_i = lax.broadcasted_iota(jnp.int32, (depth, 2 * LANES), 0)
    l_i = lax.broadcasted_iota(jnp.int32, (depth, 2 * LANES), 1)
    pick = jnp.where((r_i < members) & ((l_i == r_i) | (l_i == r_i + members)), 1.0, 0.0)
    pick = jnp.where((r_i == members) & (l_i == LANES), 1.0, pick)
    rhs = jnp.concatenate(
        [jnp.concatenate([anom, jnp.zeros((SUBS, total), jnp.float32)], axis=0), pick], axis=1)
    full = contract(lhs, rhs)
    for t in range(width):
        w_ref[t] = full[:, t * LANES:(t + 1) * LANES]

    def batch(p, carry):
        b = order_ref[p]
        o = owner_ref[b]
        mine = (mask_ref[b, tile] == 1) | (o == tile)
        mine_f = jnp.where(mine, 1.0, 0.0)
        act = []
        late = []
        for t in range(tiles):
            row = jnp.zeros((1, LANES), jnp.float32)
            row_late = jnp.zeros((1, LANES), jnp.float32)
            for q in range(per):
                other = owner_ref[order_ref[t * per + q]]
                on = (mask_ref[b, other] == 1) | (o == other)
                here = (lane1 >= q * obs) & (lane1 < (q + 1) * obs)
                row = jnp.where(here, jnp.where(on, 1.0, 0.0), row)
                row_late = jnp.where(here, jnp.where(t * per + q > p, 1.0, 0.0), row_late)
            act.append(row)
            late.append(row_late)
        act8 = [spread(a) > 0.5 for a in act]
        z_on = jnp.where(lane8 < members, mine_f, 0.0) > 0.5
        pick_w = act8 + [z_on, lane8 == 0]
        pick_b = act8 + [z_on, lane8 < 0]

        start = pl.multiple_of(p * obs, obs)
        rows = pl.ds(start, obs)
        wp = [[w_ref[t, pl.ds(pl.multiple_of(start + i * SUBS, SUBS), SUBS), :] for i in range(blocks)]
              for t in range(width)]
        shift = lax.rem(LANES - lax.rem(p, per) * obs, LANES)
        gram = w_ref[lax.div(p, per), rows, :]
        gram = pltpu.roll(gram, shift, 1)
        cols = [[jnp.broadcast_to(gram[i * SUBS:(i + 1) * SUBS, j:j + 1], (SUBS, LANES)) if i >= j // SUBS else None
                 for i in range(blocks)] for j in range(obs)]
        for k in range(obs):
            kb, ks = k // SUBS, k % SUBS
            col = cols[k]
            var = var_ref[b, k]
            pivot = spread(col[kb][ks:ks + 1, :])
            g = 1.0 / (pivot * inv + var)
            weight = g * inv
            beta = weight / (1.0 + jnp.sqrt(var * g))
            below = [None] * blocks
            below[kb] = jnp.where(sub8 > ks, col[kb], 0.0)
            for i in range(kb + 1, blocks):
                below[i] = col[i]
            for j in range(k + 1, obs):
                jb, js = j // SUBS, j % SUBS
                factor = weight * spread(col[jb][js:js + 1, :])
                for i in range(jb, blocks):
                    cols[j][i] = cols[j][i] - col[i] * factor
            for t in range(width):
                wk = spread(wp[t][kb][ks:ks + 1, :])
                both = jnp.where(pick_w[t], weight, beta) * wk
                single = jnp.where(pick_b[t], beta, 0.0) * wk
                right_ref[k:k + 1, t * LANES:(t + 1) * LANES] = both[:1]
                right_ref[obs + k:obs + k + 1, t * LANES:(t + 1) * LANES] = single[:1]
                for i in range(kb, blocks):
                    wp[t][i] = wp[t][i] - below[i] * both
        for t in range(tiles):
            for i in range(blocks):
                d = wp[t][i] * late[t]
                left_ref[i * SUBS:(i + 1) * SUBS, t * LANES:(t + 1) * LANES] = d * act[t]
                left_ref[obs + i * SUBS:obs + (i + 1) * SUBS, t * LANES:(t + 1) * LANES] = d * (1.0 - act[t])
        for i in range(blocks):
            at = pl.ds(pl.multiple_of(start + i * SUBS, SUBS), SUBS)
            z_ref[at, :] = wp[tiles][i] * mine_f
        gain = jnp.broadcast_to(right_ref[:obs, (width - 1) * LANES:(width - 1) * LANES + 1], (obs, LANES))
        v_ref[rows, :] = gain - right_ref[:obs, tiles * LANES:(tiles + 1) * LANES]

        @pl.when(p < batches - 1)
        def _():
            update = contract(left_ref[...], right_ref[...])
            for t in range(width):
                w_ref[t] = w_ref[t] - update[:, t * LANES:(t + 1) * LANES]

        return carry

    lax.fori_loop(0, batches, batch, 0)
    moved = contract(v_ref[...], z_ref[...])
    out_ref[...] = moved[members:members + half, :members]


def chain(rows, obs_value, obs_var, owner_tile, tile_mask, batch_order, tile):
    members, total = rows.shape
    half = members // 2
    obs = obs_value.shape[1]
    width = total // LANES + 2
    f32 = jnp.float32
    return pl.pallas_call(
        chain_kernel,
        out_shape=pltpu.VMEM((half, members), f32),
        in_specs=[SMEM] * 5 + [VMEM] * 2,
        out_specs=VMEM,
        scratch_shapes=[
            pltpu.VMEM((width, total, LANES), f32),
            pltpu.VMEM((2 * obs, total), f32),
            pltpu.VMEM((2 * obs, width * LANES), f32),
            pltpu.VMEM((total, LANES), f32),
            pltpu.VMEM((total, LANES), f32),
            pltpu.VMEM((obs_value.shape[0], LANES), f32),
        ],
        compiler_params=pltpu.CompilerParams(vmem_limit_bytes=8 << 20),
        name="chain",
    )(batch_order, owner_tile, tile_mask, obs_var, tile, vmem(rows), obs_value)


def left_factor(mat):
    high = mat.astype(jnp.bfloat16)
    low = (mat - high.astype(jnp.float32)).astype(jnp.bfloat16)
    return jnp.concatenate(
        [jnp.concatenate([high, high], axis=1), jnp.concatenate([low, jnp.zeros_like(low)], axis=1)], axis=0)


def apply_block(left, own, upper, lower):
    half = own.shape[0]
    x = jnp.concatenate([own, upper, lower], axis=0)
    x_high = x.astype(jnp.bfloat16)
    x_low = (x - x_high.astype(jnp.float32)).astype(jnp.bfloat16)
    y = jnp.dot(left, jnp.concatenate([x_high, x_low], axis=0), preferred_element_type=jnp.float32)
    return own + (y[:half] + y[half:])


def apply_main(mat_ref, first_ref, main_ref, ens_hbm, out_hbm, own_ref, new_ref, sem_in, sem_out):
    chans = own_ref.shape[0]
    ahead = first_ref.shape[0]
    loads = [pltpu.make_async_copy(ens_hbm.at[c], own_ref.at[c], sem_in.at[c]) for c in range(chans)]
    stores = [pltpu.make_async_copy(new_ref.at[c], out_hbm.at[c], sem_out.at[c]) for c in range(chans)]
    for load in loads:
        load.start()
    left = left_factor(mat_ref[...])
    for c in range(chans):
        oth = [first_ref[u] if u < ahead else main_ref[u - ahead] for u in (2 * c, 2 * c + 1)]
        loads[c].wait()
        new_ref[c] = apply_block(left, own_ref[c], *oth)
        stores[c].start()
    for store in stores:
        store.wait()


def apply_last(mat_ref, own_ref, last_ref, prev_hbm, out_hbm, new_ref, sem_out):
    chans = new_ref.shape[0]
    start = out_hbm.shape[0] - chans
    stores = [pltpu.make_async_copy(new_ref.at[c], out_hbm.at[start + c], sem_out.at[c]) for c in range(chans)]
    left = left_factor(mat_ref[...])
    for c in range(chans):
        own = jnp.concatenate([own_ref[2 * c], own_ref[2 * c + 1]], axis=0)
        new_ref[c] = apply_block(left, own, last_ref[2 * c], last_ref[2 * c + 1])
        stores[c].start()
    for store in stores:
        store.wait()


def apply_matrix(mat, ens, first, main, own_last, last):
    chans, half, cells = ens.shape
    tail = last.shape[0] // 2
    head = chans - tail
    f32 = jnp.float32
    state = pltpu.HBM(ens.shape, f32)
    params = pltpu.CompilerParams(vmem_limit_bytes=8 << 20)
    out = pl.pallas_call(
        apply_main,
        out_shape=state,
        in_specs=[VMEM, VMEM, VMEM, ANY],
        out_specs=ANY,
        scratch_shapes=[
            pltpu.VMEM((head, half, cells), f32),
            pltpu.VMEM((head, half, cells), f32),
            pltpu.SemaphoreType.DMA((head,)),
            pltpu.SemaphoreType.DMA((head,)),
        ],
        compiler_params=params,
        name="apply_main",
    )(vmem(mat), vmem(first), vmem(main), hbm(ens))
    return pl.pallas_call(
        apply_last,
        out_shape=state,
        in_specs=[VMEM, VMEM, VMEM, ANY],
        out_specs=ANY,
        input_output_aliases={3: 0},
        scratch_shapes=[pltpu.VMEM((tail, half, cells), f32), pltpu.SemaphoreType.DMA((tail,))],
        compiler_params=params,
        name="apply_last",
    )(vmem(mat), vmem(own_last), vmem(last), hbm(out))


def body(ensemble, obs_site, obs_value, obs_var, owner_tile, tile_mask, batch_order):
    tile = lax.axis_index("tile").astype(jnp.int32).reshape(1)
    n_tile = lax.axis_size("tile")
    swap = [(0, 1), (1, 0)]
    ens = jnp.transpose(ensemble, (1, 0, 2))
    chans, half, cells = ens.shape
    units = ens.reshape(2 * chans, half // 2, cells)
    head, tail = 1, 2
    first = lax.ppermute(first_units(units, head), "mem", swap)
    own, own_main, own_last = gather_rows(units, obs_site, owner_tile, batch_order, head, tail)
    oth = lax.ppermute(own, "mem", swap)
    main = lax.ppermute(own_main, "mem", swap)
    last = lax.ppermute(own_last, "mem", swap)
    rows = jnp.concatenate([own, oth], axis=0)
    step = 1
    while step < n_tile:
        rows = rows + lax.ppermute(rows, "tile", [(i, i ^ step) for i in range(n_tile)])
        step *= 2
    mat = chain(rows, obs_value, obs_var, owner_tile, tile_mask, batch_order, tile)
    out = apply_matrix(mat, ens, first, main, own_last, last)
    return jnp.transpose(out, (1, 0, 2))


def solution(mesh):
    return jax.shard_map(
        body,
        mesh=mesh,
        in_specs=(P("mem", None, "tile"), P(), P(), P(), P(), P(), P()),
        out_specs=P("mem", None, "tile"),
        check_vma=False,
    )
```

```python
import functools

import jax
import jax.numpy as jnp
from jax import lax
from jax.experimental import pallas as pl
from jax.experimental.pallas import tpu as pltpu
from jax.sharding import PartitionSpec as P


LANES = 128
SUBS = 8
SMEM = pl.BlockSpec(memory_space=pltpu.SMEM)
VMEM = pl.BlockSpec(memory_space=pltpu.VMEM)
ANY = pl.BlockSpec(memory_space=pl.ANY)


def hbm(x):
    return pltpu.with_memory_space_constraint(x, pltpu.HBM)


def vmem(x):
    return pltpu.with_memory_space_constraint(x, pltpu.VMEM)


def first_kernel(units_hbm, first_ref, sem):
    copy = pltpu.make_async_copy(units_hbm.at[pl.ds(0, first_ref.shape[0])], first_ref, sem)
    copy.start()
    copy.wait()


def first_units(units, count):
    return pl.pallas_call(
        first_kernel,
        out_shape=pltpu.VMEM((count,) + units.shape[1:], jnp.float32),
        in_specs=[ANY],
        out_specs=VMEM,
        scratch_shapes=[pltpu.SemaphoreType.DMA],
        name="first_units",
    )(hbm(units))


def split(value, size):
    if size & (size - 1) == 0:
        return lax.shift_right_logical(value, size.bit_length() - 1), lax.bitwise_and(value, size - 1)
    quotient = lax.div(value, size)
    return quotient, value - quotient * size


def gather_kernel(site_hbm, owner_hbm, order_hbm, units_hbm, first_ref, rows_ref, main_ref, last_ref,
                  site_ref, owner_ref, order_ref, sem):
    batches, obs = site_hbm.shape
    count, half, cells = units_hbm.shape
    per = LANES // obs
    head, middle, tail = first_ref.shape[0], main_ref.shape[0], last_ref.shape[0]
    copies = [
        pltpu.make_async_copy(owner_hbm, owner_ref, sem.at[0]),
        pltpu.make_async_copy(order_hbm, order_ref, sem.at[1]),
        pltpu.make_async_copy(site_hbm, site_ref, sem.at[2]),
        pltpu.make_async_copy(units_hbm.at[pl.ds(head, middle)], main_ref, sem.at[3]),
        pltpu.make_async_copy(units_hbm.at[pl.ds(count - tail, tail)], last_ref, sem.at[4]),
    ]
    for copy in copies:
        copy.start()
    tile = lax.axis_index("tile")
    lane = lax.broadcasted_iota(jnp.int32, (half, LANES), 1)
    rows_ref[...] = jnp.zeros_like(rows_ref)
    for copy in copies:
        copy.wait()

    def one(p, carry):
        b = order_ref[p]

        @pl.when(owner_ref[b] == tile)
        def _():
            group, place = split(p, per)
            base = place * obs
            spot = pl.ds(pl.multiple_of(group * LANES, LANES), LANES)
            acc = [rows_ref[h * half:(h + 1) * half, spot] for h in range(2)]
            for k in range(obs):
                chan, cell = split(site_ref[b, k], cells)
                _, col = split(cell, LANES)
                here = pl.ds(pl.multiple_of(cell - col, LANES), LANES)
                at = base + k
                turn = lax.bitwise_and(at - col, LANES - 1)
                mine = lane == at
                for h in range(2):
                    unit = 2 * chan + h
                    block = main_ref[jnp.clip(unit - head, 0, middle - 1), :, here]
                    early = first_ref[jnp.minimum(unit, head - 1), :, here]
                    late = last_ref[jnp.clip(unit - (count - tail), 0, tail - 1), :, here]
                    block = jnp.where(unit < head, early, jnp.where(unit >= count - tail, late, block))
                    acc[h] = jnp.where(mine, pltpu.roll(block, turn, 1), acc[h])
            for h in range(2):
                rows_ref[h * half:(h + 1) * half, spot] = acc[h]

        return carry

    lax.fori_loop(0, batches, one, 0)


def gather_rows(units, first, obs_site, owner_tile, batch_order, tail):
    batches, obs = obs_site.shape
    count, half, cells = units.shape
    f32 = jnp.float32
    return pl.pallas_call(
        gather_kernel,
        out_shape=(
            pltpu.VMEM((2 * half, batches * obs), f32),
            pltpu.VMEM((count - first.shape[0] - tail, half, cells), f32),
            pltpu.VMEM((tail, half, cells), f32),
        ),
        in_specs=[ANY] * 4 + [VMEM],
        out_specs=(VMEM, VMEM, VMEM),
        scratch_shapes=[
            pltpu.SMEM(obs_site.shape, jnp.int32),
            pltpu.SMEM(owner_tile.shape, jnp.int32),
            pltpu.SMEM(batch_order.shape, jnp.int32),
            pltpu.SemaphoreType.DMA((5,)),
        ],
        compiler_params=pltpu.CompilerParams(vmem_limit_bytes=8 << 20),
        name="gather_rows",
    )(hbm(obs_site), hbm(owner_tile), hbm(batch_order), hbm(units), vmem(first))


def spread(row):
    return jnp.broadcast_to(row, (SUBS, row.shape[1]))


def left_factor(mat):
    high = mat.astype(jnp.bfloat16)
    low = (mat - high.astype(jnp.float32)).astype(jnp.bfloat16)
    return jnp.concatenate(
        [jnp.concatenate([high, high], axis=1), jnp.concatenate([low, jnp.zeros_like(low)], axis=1)], axis=0)


def chain_kernel(order_ref, owner_ref, mask_ref, var_ref, tile_ref, raw_ref, val_ref,
                 out_ref, w_ref, left_ref, right_ref, z_ref, v_ref, val_s):
    batches, obs = val_ref.shape
    members = raw_ref.shape[0]
    half = members // 2
    total = batches * obs
    tiles = total // LANES
    per = LANES // obs
    blocks = obs // SUBS
    width = w_ref.shape[0]
    inv = 1.0 / (members - 1)
    highest = lax.Precision.HIGHEST
    contract = functools.partial(
        lax.dot_general, dimension_numbers=(((0,), (0,)), ((), ())), precision=highest,
        preferred_element_type=jnp.float32)
    lane1 = lax.broadcasted_iota(jnp.int32, (1, LANES), 1)
    lane8 = lax.broadcasted_iota(jnp.int32, (SUBS, LANES), 1)
    sub8 = lax.broadcasted_iota(jnp.int32, (SUBS, LANES), 0)
    tile = tile_ref[0]

    val_s[...] = jnp.zeros_like(val_s)
    val_s[:, :obs] = val_ref[...]
    values = []
    for t in range(tiles):
        row = jnp.zeros((1, LANES), jnp.float32)
        for q in range(per):
            one = val_s[pl.ds(order_ref[t * per + q], 1), :]
            row = row + (pltpu.roll(one, q * obs, 1) if q else one)
        values.append(row)
    values = jnp.concatenate(values, axis=1)

    raw = raw_ref[...]
    mean = jnp.sum(raw, axis=0, keepdims=True) * (1.0 / members)
    anom = raw - mean
    first = lax.broadcasted_iota(jnp.int32, (SUBS, total), 0) == 0
    lhs = jnp.concatenate([anom, jnp.where(first, values - mean, 0.0)], axis=0)
    depth = members + SUBS
    r_i = lax.broadcasted_iota(jnp.int32, (depth, 2 * LANES), 0)
    l_i = lax.broadcasted_iota(jnp.int32, (depth, 2 * LANES), 1)
    pick = jnp.where((r_i < members) & ((l_i == r_i) | (l_i == r_i + members)), 1.0, 0.0)
    pick = jnp.where((r_i == members) & (l_i == LANES), 1.0, pick)
    rhs = jnp.concatenate(
        [jnp.concatenate([anom, jnp.zeros((SUBS, total), jnp.float32)], axis=0), pick], axis=1)
    full = contract(lhs, rhs)
    for t in range(width):
        w_ref[t] = full[:, t * LANES:(t + 1) * LANES]

    def batch(p, carry):
        b = order_ref[p]
        o = owner_ref[b]
        mine = (mask_ref[b, tile] == 1) | (o == tile)
        mine_f = jnp.where(mine, 1.0, 0.0)
        act = []
        late = []
        for t in range(tiles):
            row = jnp.zeros((1, LANES), jnp.float32)
            row_late = jnp.zeros((1, LANES), jnp.float32)
            for q in range(per):
                other = owner_ref[order_ref[t * per + q]]
                on = (mask_ref[b, other] == 1) | (o == other)
                here = (lane1 >= q * obs) & (lane1 < (q + 1) * obs)
                row = jnp.where(here, jnp.where(on, 1.0, 0.0), row)
                row_late = jnp.where(here, jnp.where(t * per + q > p, 1.0, 0.0), row_late)
            act.append(row)
            late.append(row_late)
        act8 = [spread(a) > 0.5 for a in act]
        z_on = jnp.where(lane8 < members, mine_f, 0.0) > 0.5
        pick_w = act8 + [z_on, lane8 == 0]
        pick_b = act8 + [z_on, lane8 < 0]

        start = pl.multiple_of(p * obs, obs)
        rows = pl.ds(start, obs)
        wp = [[w_ref[t, pl.ds(pl.multiple_of(start + i * SUBS, SUBS), SUBS), :] for i in range(blocks)]
              for t in range(width)]
        shift = lax.rem(LANES - lax.rem(p, per) * obs, LANES)
        gram = w_ref[lax.div(p, per), rows, :] * inv
        gram = pltpu.roll(gram, shift, 1)
        cols = [[jnp.broadcast_to(gram[i * SUBS:(i + 1) * SUBS, j:j + 1], (SUBS, LANES)) if i >= j // SUBS else None
                 for i in range(blocks)] for j in range(obs)]
        for k in range(0, obs, 2):
            kb, ks = k // SUBS, k % SUBS
            one, two = cols[k], cols[k + 1]
            var1, var2 = var_ref[b, k], var_ref[b, k + 1]
            cross = spread(one[kb][ks + 1:ks + 2, :])
            total1 = spread(one[kb][ks:ks + 1, :]) + var1
            total2 = spread(two[kb][ks + 1:ks + 2, :]) + var2
            g1 = 1.0 / total1
            g2 = total1 * (1.0 / (total1 * total2 - cross * cross))
            ratio = g1 * cross
            for j in range(k + 2, obs):
                jb, js = j // SUBS, j % SUBS
                h1 = spread(one[jb][js:js + 1, :])
                h2 = spread(two[jb][js:js + 1, :])
                f2 = g2 * (h2 - ratio * h1)
                f1 = g1 * h1 - ratio * f2
                for i in range(jb, blocks):
                    cols[j][i] = cols[j][i] - (one[i] * f1 + two[i] * f2)
            moved = [two[i] - one[i] * ratio if two[i] is not None else None for i in range(blocks)]
            below1 = [None] * kb + [jnp.where(sub8 > ks, one[kb], 0.0)] + one[kb + 1:]
            below2 = [None] * kb + [jnp.where(sub8 > ks + 1, moved[kb], 0.0)] + moved[kb + 1:]
            beta1 = g1 / (1.0 + jnp.sqrt(var1 * g1))
            beta2 = g2 / (1.0 + jnp.sqrt(var2 * g2))
            for t in range(width):
                u1 = spread(wp[t][kb][ks:ks + 1, :])
                both1 = jnp.where(pick_w[t], g1, beta1) * u1
                u2 = spread(wp[t][kb][ks + 1:ks + 2, :]) - cross * both1
                both2 = jnp.where(pick_w[t], g2, beta2) * u2
                here = slice(t * LANES, (t + 1) * LANES)
                right_ref[k:k + 1, here] = both1[:1]
                right_ref[k + 1:k + 2, here] = both2[:1]
                right_ref[obs + k:obs + k + 1, here] = (jnp.where(pick_b[t], beta1, 0.0) * u1)[:1]
                right_ref[obs + k + 1:obs + k + 2, here] = (jnp.where(pick_b[t], beta2, 0.0) * u2)[:1]
                for i in range(kb, blocks):
                    wp[t][i] = wp[t][i] - (below1[i] * both1 + below2[i] * both2)
        for t in range(tiles):
            for i in range(blocks):
                d = wp[t][i] * (late[t] * inv)
                left_ref[i * SUBS:(i + 1) * SUBS, t * LANES:(t + 1) * LANES] = d * act[t]
                left_ref[obs + i * SUBS:obs + (i + 1) * SUBS, t * LANES:(t + 1) * LANES] = d * (1.0 - act[t])
        for i in range(blocks):
            at = pl.ds(pl.multiple_of(start + i * SUBS, SUBS), SUBS)
            z_ref[at, :] = wp[tiles][i] * mine_f
        gain = jnp.broadcast_to(right_ref[:obs, (width - 1) * LANES:(width - 1) * LANES + 1], (obs, LANES))
        v_ref[rows, :] = (gain - right_ref[:obs, tiles * LANES:(tiles + 1) * LANES]) * inv

        for low in range(tiles):
            @pl.when((p < batches - 1) & (lax.div(p + 1, per) == low))
            def _():
                update = contract(left_ref[:, low * LANES:], right_ref[:, low * LANES:])
                for t in range(low, width):
                    w_ref[t, low * LANES:, :] = w_ref[t, low * LANES:, :] - update[:, (t - low) * LANES:(t - low + 1) * LANES]

        return carry

    lax.fori_loop(0, batches, batch, 0)
    moved = contract(v_ref[...], z_ref[...])
    out_ref[...] = left_factor(moved[members:members + half, :members])


def chain(rows, obs_value, obs_var, owner_tile, tile_mask, batch_order, tile):
    members, total = rows.shape
    half = members // 2
    obs = obs_value.shape[1]
    width = total // LANES + 2
    f32 = jnp.float32
    return pl.pallas_call(
        chain_kernel,
        out_shape=pltpu.VMEM((2 * half, 2 * members), jnp.bfloat16),
        in_specs=[SMEM] * 5 + [VMEM] * 2,
        out_specs=VMEM,
        scratch_shapes=[
            pltpu.VMEM((width, total, LANES), f32),
            pltpu.VMEM((2 * obs, total), f32),
            pltpu.VMEM((2 * obs, width * LANES), f32),
            pltpu.VMEM((total, LANES), f32),
            pltpu.VMEM((total, LANES), f32),
            pltpu.VMEM((obs_value.shape[0], LANES), f32),
        ],
        compiler_params=pltpu.CompilerParams(vmem_limit_bytes=8 << 20),
        name="chain",
    )(batch_order, owner_tile, tile_mask, obs_var, tile, vmem(rows), obs_value)


def apply_block(left, own, upper, lower):
    half = own.shape[0]
    x = jnp.concatenate([own, upper, lower], axis=0)
    x_high = x.astype(jnp.bfloat16)
    x_low = (x - x_high.astype(jnp.float32)).astype(jnp.bfloat16)
    y = jnp.dot(left, jnp.concatenate([x_high, x_low], axis=0), preferred_element_type=jnp.float32)
    return own + (y[:half] + y[half:])


def apply_main(mat_ref, own_first_ref, own_main_ref, first_ref, main_hbm, out_hbm, main_ref, new_ref, sem_in, sem_out):
    chans = new_ref.shape[0]
    ahead = first_ref.shape[0]
    stores = [pltpu.make_async_copy(new_ref.at[c], out_hbm.at[c], sem_out.at[c]) for c in range(chans)]
    loads = []
    for c in range(chans):
        low, high = max(2 * c - ahead, 0), max(2 * c + 2 - ahead, 0)
        part = pl.ds(low, high - low)
        loads.append(pltpu.make_async_copy(main_hbm.at[part], main_ref.at[part], sem_in.at[c]) if high > low else None)
        if high > low:
            loads[c].start()
    left = mat_ref[...]

    def pair(a, b, c):
        return [a[u] if u < ahead else b[u - ahead] for u in (2 * c, 2 * c + 1)]

    for c in range(chans):
        own = jnp.concatenate(pair(own_first_ref, own_main_ref, c), axis=0)
        if loads[c] is not None:
            loads[c].wait()
        new_ref[c] = apply_block(left, own, *pair(first_ref, main_ref, c))
        stores[c].start()
    for store in stores:
        store.wait()


def apply_last(mat_ref, own_ref, last_ref, prev_hbm, out_hbm, new_ref, sem_out):
    chans = new_ref.shape[0]
    start = out_hbm.shape[0] - chans
    stores = [pltpu.make_async_copy(new_ref.at[c], out_hbm.at[start + c], sem_out.at[c]) for c in range(chans)]
    left = mat_ref[...]
    for c in range(chans):
        own = jnp.concatenate([own_ref[2 * c], own_ref[2 * c + 1]], axis=0)
        new_ref[c] = apply_block(left, own, last_ref[2 * c], last_ref[2 * c + 1])
        stores[c].start()
    for store in stores:
        store.wait()


def apply_matrix(mat, shape, own_first, own_main, own_last, first, main, last):
    chans, half, cells = shape
    tail = last.shape[0] // 2
    head = chans - tail
    f32 = jnp.float32
    state = pltpu.HBM(shape, f32)
    params = pltpu.CompilerParams(vmem_limit_bytes=8 << 20)
    out = pl.pallas_call(
        apply_main,
        out_shape=state,
        in_specs=[VMEM] * 4 + [ANY],
        out_specs=ANY,
        scratch_shapes=[
            pltpu.VMEM(main.shape, f32),
            pltpu.VMEM((head, half, cells), f32),
            pltpu.SemaphoreType.DMA((head,)),
            pltpu.SemaphoreType.DMA((head,)),
        ],
        compiler_params=params,
        name="apply_main",
    )(vmem(mat), vmem(own_first), vmem(own_main), vmem(first), hbm(main))
    return pl.pallas_call(
        apply_last,
        out_shape=state,
        in_specs=[VMEM, VMEM, VMEM, ANY],
        out_specs=ANY,
        input_output_aliases={3: 0},
        scratch_shapes=[pltpu.VMEM((tail, half, cells), f32), pltpu.SemaphoreType.DMA((tail,))],
        compiler_params=params,
        name="apply_last",
    )(vmem(mat), vmem(own_last), vmem(last), hbm(out))


def body(ensemble, obs_site, obs_value, obs_var, owner_tile, tile_mask, batch_order):
    tile = lax.axis_index("tile").astype(jnp.int32).reshape(1)
    n_tile = lax.axis_size("tile")
    swap = [(0, 1), (1, 0)]
    ens = jnp.transpose(ensemble, (1, 0, 2))
    chans, half, cells = ens.shape
    units = ens.reshape(2 * chans, half // 2, cells)
    head, tail = 2, 2
    own_first = first_units(units, head)
    first = lax.ppermute(own_first, "mem", swap)
    own, own_main, own_last = gather_rows(units, own_first, obs_site, owner_tile, batch_order, tail)
    oth = lax.ppermute(own, "mem", swap)
    main = lax.ppermute(own_main, "mem", swap)
    last = lax.ppermute(own_last, "mem", swap)
    rows = jnp.concatenate([own, oth], axis=0)
    step = 1
    while step < n_tile:
        rows = rows + lax.ppermute(rows, "tile", [(i, i ^ step) for i in range(n_tile)])
        step *= 2
    mat = chain(rows, obs_value, obs_var, owner_tile, tile_mask, batch_order, tile)
    out = apply_matrix(mat, ens.shape, own_first, own_main, own_last, first, main, last)
    return jnp.transpose(out, (1, 0, 2))


def solution(mesh):
    return jax.shard_map(
        body,
        mesh=mesh,
        in_specs=(P("mem", None, "tile"), P(), P(), P(), P(), P(), P()),
        out_specs=P("mem", None, "tile"),
        check_vma=False,
    )
```

```python
import functools

import jax
import jax.numpy as jnp
from jax import lax
from jax.experimental import pallas as pl
from jax.experimental.pallas import tpu as pltpu
from jax.sharding import PartitionSpec as P


LANES = 128
SUBS = 8
SMEM = pl.BlockSpec(memory_space=pltpu.SMEM)
VMEM = pl.BlockSpec(memory_space=pltpu.VMEM)
ANY = pl.BlockSpec(memory_space=pl.ANY)


def hbm(x):
    return pltpu.with_memory_space_constraint(x, pltpu.HBM)


def vmem(x):
    return pltpu.with_memory_space_constraint(x, pltpu.VMEM)


def first_kernel(units_hbm, first_ref, sem):
    copy = pltpu.make_async_copy(units_hbm.at[pl.ds(0, first_ref.shape[0])], first_ref, sem)
    copy.start()
    copy.wait()


def first_units(units, count):
    return pl.pallas_call(
        first_kernel,
        out_shape=pltpu.VMEM((count,) + units.shape[1:], jnp.float32),
        in_specs=[ANY],
        out_specs=VMEM,
        scratch_shapes=[pltpu.SemaphoreType.DMA],
        name="first_units",
    )(hbm(units))


def split(value, size):
    if size & (size - 1) == 0:
        return lax.shift_right_logical(value, size.bit_length() - 1), lax.bitwise_and(value, size - 1)
    quotient = lax.div(value, size)
    return quotient, value - quotient * size


def gather_kernel(site_hbm, owner_hbm, order_hbm, units_hbm, first_ref, rows_ref, main_ref, last_ref,
                  site_ref, owner_ref, order_ref, sem):
    batches, obs = site_hbm.shape
    count, half, cells = units_hbm.shape
    per = LANES // obs
    head, middle, tail = first_ref.shape[0], main_ref.shape[0], last_ref.shape[0]
    copies = [
        pltpu.make_async_copy(owner_hbm, owner_ref, sem.at[0]),
        pltpu.make_async_copy(order_hbm, order_ref, sem.at[1]),
        pltpu.make_async_copy(site_hbm, site_ref, sem.at[2]),
        pltpu.make_async_copy(units_hbm.at[pl.ds(head, middle)], main_ref, sem.at[3]),
        pltpu.make_async_copy(units_hbm.at[pl.ds(count - tail, tail)], last_ref, sem.at[4]),
    ]
    for copy in copies:
        copy.start()
    tile = lax.axis_index("tile")
    lane = lax.broadcasted_iota(jnp.int32, (half, LANES), 1)
    rows_ref[...] = jnp.zeros_like(rows_ref)
    for copy in copies:
        copy.wait()

    def one(p, carry):
        b = order_ref[p]

        @pl.when(owner_ref[b] == tile)
        def _():
            group, place = split(p, per)
            base = place * obs
            spot = pl.ds(pl.multiple_of(group * LANES, LANES), LANES)
            acc = [rows_ref[h * half:(h + 1) * half, spot] for h in range(2)]
            for k in range(obs):
                chan, cell = split(site_ref[b, k], cells)
                _, col = split(cell, LANES)
                here = pl.ds(pl.multiple_of(cell - col, LANES), LANES)
                at = base + k
                turn = lax.bitwise_and(at - col, LANES - 1)
                mine = lane == at
                for h in range(2):
                    unit = 2 * chan + h
                    block = main_ref[jnp.clip(unit - head, 0, middle - 1), :, here]
                    early = first_ref[jnp.minimum(unit, head - 1), :, here]
                    late = last_ref[jnp.clip(unit - (count - tail), 0, tail - 1), :, here]
                    block = jnp.where(unit < head, early, jnp.where(unit >= count - tail, late, block))
                    acc[h] = jnp.where(mine, pltpu.roll(block, turn, 1), acc[h])
            for h in range(2):
                rows_ref[h * half:(h + 1) * half, spot] = acc[h]

        return carry

    lax.fori_loop(0, batches, one, 0)


def gather_rows(units, first, obs_site, owner_tile, batch_order, tail):
    batches, obs = obs_site.shape
    count, half, cells = units.shape
    f32 = jnp.float32
    return pl.pallas_call(
        gather_kernel,
        out_shape=(
            pltpu.VMEM((2 * half, batches * obs), f32),
            pltpu.VMEM((count - first.shape[0] - tail, half, cells), f32),
            pltpu.VMEM((tail, half, cells), f32),
        ),
        in_specs=[ANY] * 4 + [VMEM],
        out_specs=(VMEM, VMEM, VMEM),
        scratch_shapes=[
            pltpu.SMEM(obs_site.shape, jnp.int32),
            pltpu.SMEM(owner_tile.shape, jnp.int32),
            pltpu.SMEM(batch_order.shape, jnp.int32),
            pltpu.SemaphoreType.DMA((5,)),
        ],
        compiler_params=pltpu.CompilerParams(vmem_limit_bytes=8 << 20),
        name="gather_rows",
    )(hbm(obs_site), hbm(owner_tile), hbm(batch_order), hbm(units), vmem(first))


def spread(row):
    return jnp.broadcast_to(row, (SUBS, row.shape[1]))


def left_factor(mat):
    high = mat.astype(jnp.bfloat16)
    low = (mat - high.astype(jnp.float32)).astype(jnp.bfloat16)
    return jnp.concatenate(
        [jnp.concatenate([high, high], axis=1), jnp.concatenate([low, jnp.zeros_like(low)], axis=1)], axis=0)


def chain_kernel(order_ref, owner_ref, mask_ref, var_ref, tile_ref, part_ref, back_ref, val_ref,
                 out_ref, w_ref, left_ref, right_ref, z_ref, v_ref, val_s, cov_ref):
    batches, obs = val_ref.shape
    members = part_ref.shape[0]
    half = members // 2
    total = batches * obs
    tiles = total // LANES
    per = LANES // obs
    blocks = obs // SUBS
    width = w_ref.shape[0]
    inv = 1.0 / (members - 1)
    highest = lax.Precision.HIGHEST
    contract = functools.partial(
        lax.dot_general, dimension_numbers=(((0,), (0,)), ((), ())), precision=highest,
        preferred_element_type=jnp.float32)
    lane1 = lax.broadcasted_iota(jnp.int32, (1, LANES), 1)
    lane8 = lax.broadcasted_iota(jnp.int32, (SUBS, LANES), 1)
    sub8 = lax.broadcasted_iota(jnp.int32, (SUBS, LANES), 0)
    tile = tile_ref[0]

    val_s[...] = jnp.zeros_like(val_s)
    val_s[:, :obs] = val_ref[...]
    values = []
    for t in range(tiles):
        row = jnp.zeros((1, LANES), jnp.float32)
        for q in range(per):
            one = val_s[pl.ds(order_ref[t * per + q], 1), :]
            row = row + (pltpu.roll(one, q * obs, 1) if q else one)
        values.append(row)
    values = jnp.concatenate(values, axis=1)

    part, back = part_ref[...], back_ref[...]
    even = lax.rem(tile, 2) == 0
    raw = jnp.concatenate([jnp.where(even, part, back), jnp.where(even, back, part)], axis=1)
    mean = jnp.sum(raw, axis=0, keepdims=True) * (1.0 / members)
    anom = raw - mean
    first = lax.broadcasted_iota(jnp.int32, (SUBS, total), 0) == 0
    lhs = jnp.concatenate([anom, jnp.where(first, values - mean, 0.0)], axis=0)
    depth = members + SUBS
    r_i = lax.broadcasted_iota(jnp.int32, (depth, 2 * LANES), 0)
    l_i = lax.broadcasted_iota(jnp.int32, (depth, 2 * LANES), 1)
    pick = jnp.where((r_i < members) & ((l_i == r_i) | (l_i == r_i + members)), 1.0, 0.0)
    pick = jnp.where((r_i == members) & (l_i == LANES), 1.0, pick)
    rhs = jnp.concatenate(
        [jnp.concatenate([anom, jnp.zeros((SUBS, total), jnp.float32)], axis=0), pick], axis=1)
    full = contract(lhs, rhs)
    for t in range(width):
        w_ref[t] = full[:, t * LANES:(t + 1) * LANES]

    def batch(p, carry):
        b = order_ref[p]
        o = owner_ref[b]
        mine = (mask_ref[b, tile] == 1) | (o == tile)
        mine_f = jnp.where(mine, 1.0, 0.0)
        act = []
        late = []
        for t in range(tiles):
            row = jnp.zeros((1, LANES), jnp.float32)
            row_late = jnp.zeros((1, LANES), jnp.float32)
            for q in range(per):
                other = owner_ref[order_ref[t * per + q]]
                on = (mask_ref[b, other] == 1) | (o == other)
                here = (lane1 >= q * obs) & (lane1 < (q + 1) * obs)
                row = jnp.where(here, jnp.where(on, 1.0, 0.0), row)
                row_late = jnp.where(here, jnp.where(t * per + q > p, 1.0, 0.0), row_late)
            act.append(row)
            late.append(row_late)
        act8 = [spread(a) > 0.5 for a in act]
        z_on = jnp.where(lane8 < members, mine_f, 0.0) > 0.5
        pick_w = act8 + [z_on, lane8 == 0]
        pick_b = act8 + [z_on, lane8 < 0]

        start = pl.multiple_of(p * obs, obs)
        rows = pl.ds(start, obs)
        wp = [[w_ref[t, pl.ds(pl.multiple_of(start + i * SUBS, SUBS), SUBS), :] for i in range(blocks)]
              for t in range(width)]
        shift = lax.rem(LANES - lax.rem(p, per) * obs, LANES)
        gram = w_ref[lax.div(p, per), rows, :] * inv
        gram = pltpu.roll(gram, shift, 1)
        cols = [[jnp.broadcast_to(gram[i * SUBS:(i + 1) * SUBS, j:j + 1], (SUBS, LANES)) if i >= j // SUBS else None
                 for i in range(blocks)] for j in range(obs)]
        gains, alphas = [], []
        for e in range(blocks):
            gain8 = jnp.zeros((SUBS, LANES), jnp.float32)
            ratio8 = jnp.zeros((SUBS, LANES), jnp.float32)
            scaled = []
            for r in range(SUBS):
                k = e * SUBS + r
                col = cols[k]
                var = var_ref[b, k]
                g = 1.0 / (spread(col[e][r:r + 1, :]) + var)
                gain8 = jnp.where(sub8 == r, g, gain8)
                ratio8 = jnp.where(sub8 == r, var * g, ratio8)
                scale = [None] * e + [col[i] * g for i in range(e, blocks)]
                for i in range(e, blocks):
                    cov_ref[k, i * SUBS:(i + 1) * SUBS, :] = col[i]
                for n in range(k + 1, obs):
                    if n == k + 1:
                        factor = spread(col[n // SUBS][n % SUBS:n % SUBS + 1, :])
                    else:
                        factor = cov_ref[k, pl.ds(n, SUBS, stride=0), :]
                    for i in range(n // SUBS, blocks):
                        cols[n][i] = cols[n][i] - scale[i] * factor
                scale[e] = jnp.where(sub8 > r, scale[e], 0.0)
                scaled.append(scale)
            alpha8 = 1.0 / (1.0 + jnp.sqrt(ratio8))
            gains.append(gain8)
            alphas.append(alpha8)
            for r in range(SUBS):
                alpha = spread(alpha8[r:r + 1, :])
                for t in range(width):
                    u = spread(wp[t][e][r:r + 1, :])
                    both = jnp.where(pick_w[t], u, alpha * u)
                    for i in range(e, blocks):
                        wp[t][i] = wp[t][i] - scaled[r][i] * both
        for i in range(blocks):
            gain = gains[i] * inv
            alpha = alphas[i]
            own = slice(i * SUBS, (i + 1) * SUBS)
            off = slice(obs + i * SUBS, obs + (i + 1) * SUBS)
            for t in range(width):
                here = slice(t * LANES, (t + 1) * LANES)
                reduced = alpha * wp[t][i]
                right_ref[own, here] = jnp.where(pick_w[t], wp[t][i], reduced)
                right_ref[off, here] = jnp.where(pick_b[t], reduced, 0.0)
                if t < tiles:
                    d = wp[t][i] * (late[t] * gain)
                    left_ref[own, here] = d * act[t]
                    left_ref[off, here] = d * (1.0 - act[t])
            at = pl.ds(pl.multiple_of(start + i * SUBS, SUBS), SUBS)
            z_ref[at, :] = wp[tiles][i] * mine_f
            miss = jnp.broadcast_to(wp[width - 1][i][:, :1], (SUBS, LANES))
            v_ref[at, :] = (miss - alpha * wp[tiles][i]) * gain

        for low in range(tiles):
            @pl.when((p < batches - 1) & (lax.div(p + 1, per) == low))
            def _():
                update = contract(left_ref[:, low * LANES:], right_ref[:, low * LANES:])
                for t in range(low, width):
                    w_ref[t, low * LANES:, :] = w_ref[t, low * LANES:, :] - update[:, (t - low) * LANES:(t - low + 1) * LANES]

        return carry

    lax.fori_loop(0, batches, batch, 0)
    moved = contract(v_ref[...], z_ref[...])
    out_ref[...] = left_factor(moved[members:members + half, :members])


def chain(part, back, obs_value, obs_var, owner_tile, tile_mask, batch_order, tile):
    members, total = part.shape[0], 2 * part.shape[1]
    half = members // 2
    obs = obs_value.shape[1]
    width = total // LANES + 2
    f32 = jnp.float32
    return pl.pallas_call(
        chain_kernel,
        out_shape=pltpu.VMEM((2 * half, 2 * members), jnp.bfloat16),
        in_specs=[SMEM] * 5 + [VMEM] * 3,
        out_specs=VMEM,
        scratch_shapes=[
            pltpu.VMEM((width, total, LANES), f32),
            pltpu.VMEM((2 * obs, total), f32),
            pltpu.VMEM((2 * obs, width * LANES), f32),
            pltpu.VMEM((total, LANES), f32),
            pltpu.VMEM((total, LANES), f32),
            pltpu.VMEM((obs_value.shape[0], LANES), f32),
            pltpu.VMEM((obs, obs, LANES), f32),
        ],
        compiler_params=pltpu.CompilerParams(vmem_limit_bytes=8 << 20),
        name="chain",
    )(batch_order, owner_tile, tile_mask, obs_var, tile, vmem(part), vmem(back), obs_value)


def apply_block(left, own, upper, lower):
    half = own.shape[0]
    x = jnp.concatenate([own, upper, lower], axis=0)
    x_high = x.astype(jnp.bfloat16)
    x_low = (x - x_high.astype(jnp.float32)).astype(jnp.bfloat16)
    y = jnp.dot(left, jnp.concatenate([x_high, x_low], axis=0), preferred_element_type=jnp.float32)
    return own + (y[:half] + y[half:])


def apply_main(mat_ref, own_first_ref, own_main_ref, first_ref, main_ref, out_hbm, new_ref, sem_out):
    chans = new_ref.shape[0]
    ahead = first_ref.shape[0]
    stores = [pltpu.make_async_copy(new_ref.at[c], out_hbm.at[c], sem_out.at[c]) for c in range(chans)]
    left = mat_ref[...]

    def pair(a, b, c):
        return [a[u] if u < ahead else b[u - ahead] for u in (2 * c, 2 * c + 1)]

    for c in range(chans):
        own = jnp.concatenate(pair(own_first_ref, own_main_ref, c), axis=0)
        new_ref[c] = apply_block(left, own, *pair(first_ref, main_ref, c))
        stores[c].start()
    for store in stores:
        store.wait()


def apply_last(mat_ref, own_ref, last_ref, prev_hbm, out_hbm, new_ref, sem_out):
    chans = new_ref.shape[0]
    start = out_hbm.shape[0] - chans
    stores = [pltpu.make_async_copy(new_ref.at[c], out_hbm.at[start + c], sem_out.at[c]) for c in range(chans)]
    left = mat_ref[...]
    for c in range(chans):
        own = jnp.concatenate([own_ref[2 * c], own_ref[2 * c + 1]], axis=0)
        new_ref[c] = apply_block(left, own, last_ref[2 * c], last_ref[2 * c + 1])
        stores[c].start()
    for store in stores:
        store.wait()


def apply_matrix(mat, shape, own_first, own_main, own_last, first, main, last):
    chans, half, cells = shape
    tail = last.shape[0] // 2
    head = chans - tail
    f32 = jnp.float32
    state = pltpu.HBM(shape, f32)
    params = pltpu.CompilerParams(vmem_limit_bytes=8 << 20)
    out = pl.pallas_call(
        apply_main,
        out_shape=state,
        in_specs=[VMEM] * 5,
        out_specs=ANY,
        scratch_shapes=[pltpu.VMEM((head, half, cells), f32), pltpu.SemaphoreType.DMA((head,))],
        compiler_params=params,
        name="apply_main",
    )(vmem(mat), vmem(own_first), vmem(own_main), vmem(first), vmem(main))
    return pl.pallas_call(
        apply_last,
        out_shape=state,
        in_specs=[VMEM, VMEM, VMEM, ANY],
        out_specs=ANY,
        input_output_aliases={3: 0},
        scratch_shapes=[pltpu.VMEM((tail, half, cells), f32), pltpu.SemaphoreType.DMA((tail,))],
        compiler_params=params,
        name="apply_last",
    )(vmem(mat), vmem(own_last), vmem(last), hbm(out))


def body(ensemble, obs_site, obs_value, obs_var, owner_tile, tile_mask, batch_order):
    tile = lax.axis_index("tile").astype(jnp.int32).reshape(1)
    n_tile = lax.axis_size("tile")
    swap = [(0, 1), (1, 0)]
    ens = jnp.transpose(ensemble, (1, 0, 2))
    chans, half, cells = ens.shape
    units = ens.reshape(2 * chans, half // 2, cells)
    head, tail = 3, 2

    def across(x, step):
        return lax.ppermute(x, "tile", [(i, i ^ step) for i in range(n_tile)])

    own_first = first_units(units, head)
    first = lax.ppermute(own_first, "mem", swap)
    own, own_main, own_last = gather_rows(units, own_first, obs_site, owner_tile, batch_order, tail)
    own = own + across(own, 1)
    cut = own.shape[1] // 2
    own = jnp.where(lax.rem(tile[0], 2) == 0, own[:, :cut], own[:, cut:])
    oth = lax.ppermute(own, "mem", swap)
    main = lax.ppermute(own_main, "mem", swap)
    last = lax.ppermute(own_last, "mem", swap)
    part = jnp.concatenate([own, oth], axis=0)
    step = 2
    while step < n_tile:
        part = part + across(part, step)
        step *= 2
    back = lax.ppermute(part, "tile", [(i, i ^ 1) for i in range(n_tile)])
    mat = chain(part, back, obs_value, obs_var, owner_tile, tile_mask, batch_order, tile)
    out = apply_matrix(mat, ens.shape, own_first, own_main, own_last, first, main, last)
    return jnp.transpose(out, (1, 0, 2))


def solution(mesh):
    return jax.shard_map(
        body,
        mesh=mesh,
        in_specs=(P("mem", None, "tile"), P(), P(), P(), P(), P(), P()),
        out_specs=P("mem", None, "tile"),
        check_vma=False,
    )
```

```python
import functools

import jax
import jax.numpy as jnp
from jax import lax
from jax.experimental import pallas as pl
from jax.experimental.pallas import tpu as pltpu
from jax.sharding import PartitionSpec as P


LANES = 128
SUBS = 8
SMEM = pl.BlockSpec(memory_space=pltpu.SMEM)
VMEM = pl.BlockSpec(memory_space=pltpu.VMEM)
ANY = pl.BlockSpec(memory_space=pl.ANY)


def hbm(x):
    return pltpu.with_memory_space_constraint(x, pltpu.HBM)


def vmem(x):
    return pltpu.with_memory_space_constraint(x, pltpu.VMEM)


def first_kernel(units_hbm, first_ref, sem):
    copy = pltpu.make_async_copy(units_hbm.at[pl.ds(0, first_ref.shape[0])], first_ref, sem)
    copy.start()
    copy.wait()


def first_units(units, count):
    return pl.pallas_call(
        first_kernel,
        out_shape=pltpu.VMEM((count,) + units.shape[1:], jnp.float32),
        in_specs=[ANY],
        out_specs=VMEM,
        scratch_shapes=[pltpu.SemaphoreType.DMA],
        name="first_units",
    )(hbm(units))


def split(value, size):
    if size & (size - 1) == 0:
        return lax.shift_right_logical(value, size.bit_length() - 1), lax.bitwise_and(value, size - 1)
    quotient = lax.div(value, size)
    return quotient, value - quotient * size


def gather_kernel(site_hbm, owner_hbm, order_hbm, units_hbm, first_ref, rows_ref, main_ref, last_ref,
                  site_ref, owner_ref, order_ref, sem):
    batches, obs = site_hbm.shape
    count, half, cells = units_hbm.shape
    per = LANES // obs
    head, middle, tail = first_ref.shape[0], main_ref.shape[0], last_ref.shape[0]
    copies = [
        pltpu.make_async_copy(owner_hbm, owner_ref, sem.at[0]),
        pltpu.make_async_copy(order_hbm, order_ref, sem.at[1]),
        pltpu.make_async_copy(site_hbm, site_ref, sem.at[2]),
        pltpu.make_async_copy(units_hbm.at[pl.ds(head, middle)], main_ref, sem.at[3]),
        pltpu.make_async_copy(units_hbm.at[pl.ds(count - tail, tail)], last_ref, sem.at[4]),
    ]
    for copy in copies:
        copy.start()
    tile = lax.axis_index("tile")
    lane = lax.broadcasted_iota(jnp.int32, (half, LANES), 1)
    rows_ref[...] = jnp.zeros_like(rows_ref)
    for copy in copies:
        copy.wait()

    def one(p, carry):
        b = order_ref[p]

        @pl.when(owner_ref[b] == tile)
        def _():
            group, place = split(p, per)
            base = place * obs
            spot = pl.ds(pl.multiple_of(group * LANES, LANES), LANES)
            acc = [rows_ref[h * half:(h + 1) * half, spot] for h in range(2)]
            for k in range(obs):
                chan, cell = split(site_ref[b, k], cells)
                _, col = split(cell, LANES)
                here = pl.ds(pl.multiple_of(cell - col, LANES), LANES)
                at = base + k
                turn = lax.bitwise_and(at - col, LANES - 1)
                mine = lane == at
                for h in range(2):
                    unit = 2 * chan + h
                    block = main_ref[jnp.clip(unit - head, 0, middle - 1), :, here]
                    early = first_ref[jnp.minimum(unit, head - 1), :, here]
                    late = last_ref[jnp.clip(unit - (count - tail), 0, tail - 1), :, here]
                    block = jnp.where(unit < head, early, jnp.where(unit >= count - tail, late, block))
                    acc[h] = jnp.where(mine, pltpu.roll(block, turn, 1), acc[h])
            for h in range(2):
                rows_ref[h * half:(h + 1) * half, spot] = acc[h]

        return carry

    lax.fori_loop(0, batches, one, 0)


def gather_rows(units, first, obs_site, owner_tile, batch_order, tail):
    batches, obs = obs_site.shape
    count, half, cells = units.shape
    f32 = jnp.float32
    return pl.pallas_call(
        gather_kernel,
        out_shape=(
            pltpu.VMEM((2 * half, batches * obs), f32),
            pltpu.VMEM((count - first.shape[0] - tail, half, cells), f32),
            pltpu.VMEM((tail, half, cells), f32),
        ),
        in_specs=[ANY] * 4 + [VMEM],
        out_specs=(VMEM, VMEM, VMEM),
        scratch_shapes=[
            pltpu.SMEM(obs_site.shape, jnp.int32),
            pltpu.SMEM(owner_tile.shape, jnp.int32),
            pltpu.SMEM(batch_order.shape, jnp.int32),
            pltpu.SemaphoreType.DMA((5,)),
        ],
        compiler_params=pltpu.CompilerParams(vmem_limit_bytes=8 << 20),
        name="gather_rows",
    )(hbm(obs_site), hbm(owner_tile), hbm(batch_order), hbm(units), vmem(first))


def spread(row):
    return jnp.broadcast_to(row, (SUBS, row.shape[1]))


def thirds(x):
    parts = []
    for _ in range(3):
        parts.append(x.astype(jnp.bfloat16))
        x = x - parts[-1].astype(jnp.float32)
    return parts


def left_factor(mat):
    high, mid, low = thirds(mat)
    zero = jnp.zeros_like(low)
    return jnp.concatenate([
        jnp.concatenate([high, high, high], axis=1),
        jnp.concatenate([mid, mid, zero], axis=1),
        jnp.concatenate([low, zero, zero], axis=1),
    ], axis=0)


def chain_kernel(order_ref, owner_ref, mask_ref, var_ref, tile_ref, part_ref, back_ref, val_ref,
                 out_ref, w_ref, left_ref, right_ref, z_ref, v_ref, val_s, cov_ref):
    batches, obs = val_ref.shape
    members = part_ref.shape[0]
    half = members // 2
    total = batches * obs
    tiles = total // LANES
    per = LANES // obs
    blocks = obs // SUBS
    width = w_ref.shape[0]
    inv = 1.0 / (members - 1)
    highest = lax.Precision.HIGHEST
    contract = functools.partial(
        lax.dot_general, dimension_numbers=(((0,), (0,)), ((), ())), precision=highest,
        preferred_element_type=jnp.float32)
    lane1 = lax.broadcasted_iota(jnp.int32, (1, LANES), 1)
    lane8 = lax.broadcasted_iota(jnp.int32, (SUBS, LANES), 1)
    sub8 = lax.broadcasted_iota(jnp.int32, (SUBS, LANES), 0)
    tile = tile_ref[0]

    val_s[...] = jnp.zeros_like(val_s)
    val_s[:, :obs] = val_ref[...]
    values = []
    for t in range(tiles):
        row = jnp.zeros((1, LANES), jnp.float32)
        for q in range(per):
            one = val_s[pl.ds(order_ref[t * per + q], 1), :]
            row = row + (pltpu.roll(one, q * obs, 1) if q else one)
        values.append(row)
    values = jnp.concatenate(values, axis=1)

    part, back = part_ref[...], back_ref[...]
    even = lax.rem(tile, 2) == 0
    raw = jnp.concatenate([jnp.where(even, part, back), jnp.where(even, back, part)], axis=1)
    mean = jnp.sum(raw, axis=0, keepdims=True) * (1.0 / members)
    anom = raw - mean
    first = lax.broadcasted_iota(jnp.int32, (SUBS, total), 0) == 0
    lhs = jnp.concatenate([anom, jnp.where(first, values - mean, 0.0)], axis=0)
    depth = members + SUBS
    r_i = lax.broadcasted_iota(jnp.int32, (depth, 2 * LANES), 0)
    l_i = lax.broadcasted_iota(jnp.int32, (depth, 2 * LANES), 1)
    pick = jnp.where((r_i < members) & ((l_i == r_i) | (l_i == r_i + members)), 1.0, 0.0)
    pick = jnp.where((r_i == members) & (l_i == LANES), 1.0, pick)
    rhs = jnp.concatenate(
        [jnp.concatenate([anom, jnp.zeros((SUBS, total), jnp.float32)], axis=0), pick], axis=1)
    full = contract(lhs, rhs)
    for t in range(width):
        w_ref[t] = full[:, t * LANES:(t + 1) * LANES]

    def batch(p, carry):
        b = order_ref[p]
        o = owner_ref[b]
        mine = (mask_ref[b, tile] == 1) | (o == tile)
        mine_f = jnp.where(mine, 1.0, 0.0)
        act = []
        late = []
        for t in range(tiles):
            row = jnp.zeros((1, LANES), jnp.float32)
            row_late = jnp.zeros((1, LANES), jnp.float32)
            for q in range(per):
                other = owner_ref[order_ref[t * per + q]]
                on = (mask_ref[b, other] == 1) | (o == other)
                here = (lane1 >= q * obs) & (lane1 < (q + 1) * obs)
                row = jnp.where(here, jnp.where(on, 1.0, 0.0), row)
                row_late = jnp.where(here, jnp.where(t * per + q > p, 1.0, 0.0), row_late)
            act.append(row)
            late.append(row_late)
        act8 = [spread(a) > 0.5 for a in act]
        z_on = jnp.where(lane8 < members, mine_f, 0.0) > 0.5
        pick_w = act8 + [z_on, lane8 == 0]
        pick_b = act8 + [z_on, lane8 < 0]

        start = pl.multiple_of(p * obs, obs)
        rows = pl.ds(start, obs)
        wp = [[w_ref[t, pl.ds(pl.multiple_of(start + i * SUBS, SUBS), SUBS), :] for i in range(blocks)]
              for t in range(width)]
        shift = lax.rem(LANES - lax.rem(p, per) * obs, LANES)
        gram = w_ref[lax.div(p, per), rows, :] * inv
        gram = pltpu.roll(gram, shift, 1)
        cols = [[jnp.broadcast_to(gram[i * SUBS:(i + 1) * SUBS, j:j + 1], (SUBS, LANES)) if i >= j // SUBS else None
                 for i in range(blocks)] for j in range(obs)]
        gains, alphas = [], []
        for e in range(blocks):
            gain8 = jnp.zeros((SUBS, LANES), jnp.float32)
            ratio8 = jnp.zeros((SUBS, LANES), jnp.float32)
            scaled = []
            for r in range(SUBS):
                k = e * SUBS + r
                col = cols[k]
                var = var_ref[b, k]
                g = 1.0 / (spread(col[e][r:r + 1, :]) + var)
                gain8 = jnp.where(sub8 == r, g, gain8)
                ratio8 = jnp.where(sub8 == r, var * g, ratio8)
                scale = [None] * e + [col[i] * g for i in range(e, blocks)]
                for i in range(e, blocks):
                    cov_ref[k, i * SUBS:(i + 1) * SUBS, :] = col[i]
                for n in range(k + 1, obs):
                    if n == k + 1:
                        factor = spread(col[n // SUBS][n % SUBS:n % SUBS + 1, :])
                    else:
                        factor = cov_ref[k, pl.ds(n, SUBS, stride=0), :]
                    for i in range(n // SUBS, blocks):
                        cols[n][i] = cols[n][i] - scale[i] * factor
                scale[e] = jnp.where(sub8 > r, scale[e], 0.0)
                scaled.append(scale)
            alpha8 = 1.0 / (1.0 + jnp.sqrt(ratio8))
            gains.append(gain8)
            alphas.append(alpha8)
            for r in range(SUBS):
                alpha = spread(alpha8[r:r + 1, :])
                for t in range(width):
                    u = spread(wp[t][e][r:r + 1, :])
                    both = jnp.where(pick_w[t], u, alpha * u)
                    for i in range(e, blocks):
                        wp[t][i] = wp[t][i] - scaled[r][i] * both
        for i in range(blocks):
            gain = gains[i] * inv
            alpha = alphas[i]
            own = slice(i * SUBS, (i + 1) * SUBS)
            off = slice(obs + i * SUBS, obs + (i + 1) * SUBS)
            for t in range(width):
                here = slice(t * LANES, (t + 1) * LANES)
                reduced = alpha * wp[t][i]
                right_ref[own, here] = jnp.where(pick_w[t], wp[t][i], reduced)
                right_ref[off, here] = jnp.where(pick_b[t], reduced, 0.0)
                if t < tiles:
                    d = wp[t][i] * (late[t] * gain)
                    left_ref[own, here] = d * act[t]
                    left_ref[off, here] = d * (1.0 - act[t])
            at = pl.ds(pl.multiple_of(start + i * SUBS, SUBS), SUBS)
            z_ref[at, :] = wp[tiles][i] * mine_f
            miss = jnp.broadcast_to(wp[width - 1][i][:, :1], (SUBS, LANES))
            v_ref[at, :] = (miss - alpha * wp[tiles][i]) * gain

        for low in range(tiles):
            @pl.when((p < batches - 1) & (lax.div(p + 1, per) == low))
            def _():
                update = contract(left_ref[:, low * LANES:], right_ref[:, low * LANES:])
                for t in range(low, width):
                    w_ref[t, low * LANES:, :] = w_ref[t, low * LANES:, :] - update[:, (t - low) * LANES:(t - low + 1) * LANES]

        return carry

    lax.fori_loop(0, batches, batch, 0)
    moved = contract(v_ref[...], z_ref[...])
    out_ref[...] = left_factor(moved[members:members + half, :members])


def chain(part, back, obs_value, obs_var, owner_tile, tile_mask, batch_order, tile):
    members, total = part.shape[0], 2 * part.shape[1]
    half = members // 2
    obs = obs_value.shape[1]
    width = total // LANES + 2
    f32 = jnp.float32
    return pl.pallas_call(
        chain_kernel,
        out_shape=pltpu.VMEM((3 * half, 3 * members), jnp.bfloat16),
        in_specs=[SMEM] * 5 + [VMEM] * 3,
        out_specs=VMEM,
        scratch_shapes=[
            pltpu.VMEM((width, total, LANES), f32),
            pltpu.VMEM((2 * obs, total), f32),
            pltpu.VMEM((2 * obs, width * LANES), f32),
            pltpu.VMEM((total, LANES), f32),
            pltpu.VMEM((total, LANES), f32),
            pltpu.VMEM((obs_value.shape[0], LANES), f32),
            pltpu.VMEM((obs, obs, LANES), f32),
        ],
        compiler_params=pltpu.CompilerParams(vmem_limit_bytes=8 << 20),
        name="chain",
    )(batch_order, owner_tile, tile_mask, obs_var, tile, vmem(part), vmem(back), obs_value)


def apply_block(left, own, upper, lower):
    half = own.shape[0]
    x = jnp.concatenate(thirds(jnp.concatenate([own, upper, lower], axis=0)), axis=0)
    y = jnp.dot(left, x, preferred_element_type=jnp.float32)
    return own + ((y[2 * half:] + y[half:2 * half]) + y[:half])


def apply_main(mat_ref, own_first_ref, own_main_ref, first_ref, main_ref, out_hbm, new_ref, sem_out):
    chans = new_ref.shape[0]
    ahead = first_ref.shape[0]
    stores = [pltpu.make_async_copy(new_ref.at[c], out_hbm.at[c], sem_out.at[c]) for c in range(chans)]
    left = mat_ref[...]

    def pair(a, b, c):
        return [a[u] if u < ahead else b[u - ahead] for u in (2 * c, 2 * c + 1)]

    for c in range(chans):
        own = jnp.concatenate(pair(own_first_ref, own_main_ref, c), axis=0)
        new_ref[c] = apply_block(left, own, *pair(first_ref, main_ref, c))
        stores[c].start()
    for store in stores:
        store.wait()


def apply_last(mat_ref, own_ref, last_ref, prev_hbm, out_hbm, new_ref, sem_out):
    chans = new_ref.shape[0]
    start = out_hbm.shape[0] - chans
    stores = [pltpu.make_async_copy(new_ref.at[c], out_hbm.at[start + c], sem_out.at[c]) for c in range(chans)]
    left = mat_ref[...]
    for c in range(chans):
        own = jnp.concatenate([own_ref[2 * c], own_ref[2 * c + 1]], axis=0)
        new_ref[c] = apply_block(left, own, last_ref[2 * c], last_ref[2 * c + 1])
        stores[c].start()
    for store in stores:
        store.wait()


def apply_matrix(mat, shape, own_first, own_main, own_last, first, main, last):
    chans, half, cells = shape
    tail = last.shape[0] // 2
    head = chans - tail
    f32 = jnp.float32
    state = pltpu.HBM(shape, f32)
    params = pltpu.CompilerParams(vmem_limit_bytes=8 << 20)
    out = pl.pallas_call(
        apply_main,
        out_shape=state,
        in_specs=[VMEM] * 5,
        out_specs=ANY,
        scratch_shapes=[pltpu.VMEM((head, half, cells), f32), pltpu.SemaphoreType.DMA((head,))],
        compiler_params=params,
        name="apply_main",
    )(vmem(mat), vmem(own_first), vmem(own_main), vmem(first), vmem(main))
    return pl.pallas_call(
        apply_last,
        out_shape=state,
        in_specs=[VMEM, VMEM, VMEM, ANY],
        out_specs=ANY,
        input_output_aliases={3: 0},
        scratch_shapes=[pltpu.VMEM((tail, half, cells), f32), pltpu.SemaphoreType.DMA((tail,))],
        compiler_params=params,
        name="apply_last",
    )(vmem(mat), vmem(own_last), vmem(last), hbm(out))


def body(ensemble, obs_site, obs_value, obs_var, owner_tile, tile_mask, batch_order):
    tile = lax.axis_index("tile").astype(jnp.int32).reshape(1)
    n_tile = lax.axis_size("tile")
    swap = [(0, 1), (1, 0)]
    ens = jnp.transpose(ensemble, (1, 0, 2))
    chans, half, cells = ens.shape
    units = ens.reshape(2 * chans, half // 2, cells)
    head, tail = 3, 2

    def across(x, step):
        return lax.ppermute(x, "tile", [(i, i ^ step) for i in range(n_tile)])

    own_first = first_units(units, head)
    first = lax.ppermute(own_first, "mem", swap)
    own, own_main, own_last = gather_rows(units, own_first, obs_site, owner_tile, batch_order, tail)
    own = own + across(own, 1)
    cut = own.shape[1] // 2
    own = jnp.where(lax.rem(tile[0], 2) == 0, own[:, :cut], own[:, cut:])
    oth = lax.ppermute(own, "mem", swap)
    main = lax.ppermute(own_main, "mem", swap)
    last = lax.ppermute(own_last, "mem", swap)
    part = jnp.concatenate([own, oth], axis=0)
    step = 2
    while step < n_tile:
        part = part + across(part, step)
        step *= 2
    back = lax.ppermute(part, "tile", [(i, i ^ 1) for i in range(n_tile)])
    mat = chain(part, back, obs_value, obs_var, owner_tile, tile_mask, batch_order, tile)
    out = apply_matrix(mat, ens.shape, own_first, own_main, own_last, first, main, last)
    return jnp.transpose(out, (1, 0, 2))


def solution(mesh):
    return jax.shard_map(
        body,
        mesh=mesh,
        in_specs=(P("mem", None, "tile"), P(), P(), P(), P(), P(), P()),
        out_specs=P("mem", None, "tile"),
        check_vma=False,
    )
```

```python
import functools

import jax
import jax.numpy as jnp
from jax import lax
from jax.experimental import pallas as pl
from jax.experimental.pallas import tpu as pltpu
from jax.sharding import PartitionSpec as P


LANES = 128
SUBS = 8
SMEM = pl.BlockSpec(memory_space=pltpu.SMEM)
VMEM = pl.BlockSpec(memory_space=pltpu.VMEM)
ANY = pl.BlockSpec(memory_space=pl.ANY)


def hbm(x):
    return pltpu.with_memory_space_constraint(x, pltpu.HBM)


def vmem(x):
    return pltpu.with_memory_space_constraint(x, pltpu.VMEM)


def first_kernel(units_hbm, first_ref, sem):
    copy = pltpu.make_async_copy(units_hbm.at[pl.ds(0, first_ref.shape[0])], first_ref, sem)
    copy.start()
    copy.wait()


def first_units(units, count):
    return pl.pallas_call(
        first_kernel,
        out_shape=pltpu.VMEM((count,) + units.shape[1:], jnp.float32),
        in_specs=[ANY],
        out_specs=VMEM,
        scratch_shapes=[pltpu.SemaphoreType.DMA],
        name="first_units",
    )(hbm(units))


def split(value, size):
    if size & (size - 1) == 0:
        return lax.shift_right_logical(value, size.bit_length() - 1), lax.bitwise_and(value, size - 1)
    quotient = lax.div(value, size)
    return quotient, value - quotient * size


def gather_kernel(site_hbm, owner_hbm, order_hbm, units_hbm, first_ref, rows_ref, main_ref, last_ref,
                  site_ref, owner_ref, order_ref, sem):
    batches, obs = site_hbm.shape
    count, half, cells = units_hbm.shape
    per = LANES // obs
    head, middle, tail = first_ref.shape[0], main_ref.shape[0], last_ref.shape[0]
    copies = [
        pltpu.make_async_copy(owner_hbm, owner_ref, sem.at[0]),
        pltpu.make_async_copy(order_hbm, order_ref, sem.at[1]),
        pltpu.make_async_copy(site_hbm, site_ref, sem.at[2]),
        pltpu.make_async_copy(units_hbm.at[pl.ds(head, middle)], main_ref, sem.at[3]),
        pltpu.make_async_copy(units_hbm.at[pl.ds(count - tail, tail)], last_ref, sem.at[4]),
    ]
    for copy in copies:
        copy.start()
    tile = lax.axis_index("tile")
    lane = lax.broadcasted_iota(jnp.int32, (half, LANES), 1)
    rows_ref[...] = jnp.zeros_like(rows_ref)
    for copy in copies:
        copy.wait()

    def one(p, carry):
        b = order_ref[p]

        @pl.when(owner_ref[b] == tile)
        def _():
            group, place = split(p, per)
            base = place * obs
            spot = pl.ds(pl.multiple_of(group * LANES, LANES), LANES)
            acc = [rows_ref[h * half:(h + 1) * half, spot] for h in range(2)]
            for k in range(obs):
                chan, cell = split(site_ref[b, k], cells)
                _, col = split(cell, LANES)
                here = pl.ds(pl.multiple_of(cell - col, LANES), LANES)
                at = base + k
                turn = lax.bitwise_and(at - col, LANES - 1)
                mine = lane == at
                for h in range(2):
                    unit = 2 * chan + h
                    block = main_ref[jnp.clip(unit - head, 0, middle - 1), :, here]
                    early = first_ref[jnp.minimum(unit, head - 1), :, here]
                    late = last_ref[jnp.clip(unit - (count - tail), 0, tail - 1), :, here]
                    block = jnp.where(unit < head, early, jnp.where(unit >= count - tail, late, block))
                    acc[h] = jnp.where(mine, pltpu.roll(block, turn, 1), acc[h])
            for h in range(2):
                rows_ref[h * half:(h + 1) * half, spot] = acc[h]

        return carry

    lax.fori_loop(0, batches, one, 0)


def gather_rows(units, first, obs_site, owner_tile, batch_order, tail):
    batches, obs = obs_site.shape
    count, half, cells = units.shape
    f32 = jnp.float32
    return pl.pallas_call(
        gather_kernel,
        out_shape=(
            pltpu.VMEM((2 * half, batches * obs), f32),
            pltpu.VMEM((count - first.shape[0] - tail, half, cells), f32),
            pltpu.VMEM((tail, half, cells), f32),
        ),
        in_specs=[ANY] * 4 + [VMEM],
        out_specs=(VMEM, VMEM, VMEM),
        scratch_shapes=[
            pltpu.SMEM(obs_site.shape, jnp.int32),
            pltpu.SMEM(owner_tile.shape, jnp.int32),
            pltpu.SMEM(batch_order.shape, jnp.int32),
            pltpu.SemaphoreType.DMA((5,)),
        ],
        compiler_params=pltpu.CompilerParams(vmem_limit_bytes=8 << 20),
        name="gather_rows",
    )(hbm(obs_site), hbm(owner_tile), hbm(batch_order), hbm(units), vmem(first))


def spread(row):
    return jnp.broadcast_to(row, (SUBS, row.shape[1]))


def thirds(x):
    parts = []
    for _ in range(3):
        parts.append(x.astype(jnp.bfloat16))
        x = x - parts[-1].astype(jnp.float32)
    return parts


def left_factor(mat):
    high, mid, low = thirds(mat)
    zero = jnp.zeros_like(low)
    return jnp.concatenate([
        jnp.concatenate([high, high, high], axis=1),
        jnp.concatenate([mid, mid, zero], axis=1),
        jnp.concatenate([low, zero, zero], axis=1),
    ], axis=0)


def chain_kernel(order_ref, owner_ref, mask_ref, var_ref, tile_ref, part_ref, back_ref, val_ref,
                 out_ref, mine_ref, theirs_ref, w_ref, left_ref, right_ref, z_ref, v_ref, val_s, cov_ref):
    batches, obs = val_ref.shape
    members = part_ref.shape[0]
    half = members // 2
    total = batches * obs
    tiles = total // LANES
    per = LANES // obs
    blocks = obs // SUBS
    width = w_ref.shape[0]
    inv = 1.0 / (members - 1)
    highest = lax.Precision.HIGHEST
    contract = functools.partial(
        lax.dot_general, dimension_numbers=(((0,), (0,)), ((), ())), precision=highest,
        preferred_element_type=jnp.float32)
    lane1 = lax.broadcasted_iota(jnp.int32, (1, LANES), 1)
    lane8 = lax.broadcasted_iota(jnp.int32, (SUBS, LANES), 1)
    sub8 = lax.broadcasted_iota(jnp.int32, (SUBS, LANES), 0)
    tile = tile_ref[0]

    val_s[...] = jnp.zeros_like(val_s)
    val_s[:, :obs] = val_ref[...]
    values = []
    for t in range(tiles):
        row = jnp.zeros((1, LANES), jnp.float32)
        for q in range(per):
            one = val_s[pl.ds(order_ref[t * per + q], 1), :]
            row = row + (pltpu.roll(one, q * obs, 1) if q else one)
        values.append(row)
    values = jnp.concatenate(values, axis=1)

    part, back = part_ref[...], back_ref[...]
    even = lax.rem(tile, 2) == 0
    raw = jnp.concatenate([jnp.where(even, part, back), jnp.where(even, back, part)], axis=1)
    mean = jnp.sum(raw, axis=0, keepdims=True) * (1.0 / members)
    anom = raw - mean
    first = lax.broadcasted_iota(jnp.int32, (SUBS, total), 0) == 0
    lhs = jnp.concatenate([anom, jnp.where(first, values - mean, 0.0)], axis=0)
    depth = members + SUBS
    r_i = lax.broadcasted_iota(jnp.int32, (depth, 2 * LANES), 0)
    l_i = lax.broadcasted_iota(jnp.int32, (depth, 2 * LANES), 1)
    pick = jnp.where((r_i < members) & ((l_i == r_i) | (l_i == r_i + members)), 1.0, 0.0)
    pick = jnp.where((r_i == members) & (l_i == LANES), 1.0, pick)
    rhs = jnp.concatenate(
        [jnp.concatenate([anom, jnp.zeros((SUBS, total), jnp.float32)], axis=0), pick], axis=1)
    full = contract(lhs, rhs)
    for t in range(width):
        w_ref[t] = full[:, t * LANES:(t + 1) * LANES]

    def batch(p, carry):
        b = order_ref[p]
        o = owner_ref[b]
        mine = (mask_ref[b, tile] == 1) | (o == tile)
        mine_f = jnp.where(mine, 1.0, 0.0)
        act = []
        late = []
        for t in range(tiles):
            row = jnp.zeros((1, LANES), jnp.float32)
            row_late = jnp.zeros((1, LANES), jnp.float32)
            for q in range(per):
                other = owner_ref[order_ref[t * per + q]]
                on = (mask_ref[b, other] == 1) | (o == other)
                here = (lane1 >= q * obs) & (lane1 < (q + 1) * obs)
                row = jnp.where(here, jnp.where(on, 1.0, 0.0), row)
                row_late = jnp.where(here, jnp.where(t * per + q > p, 1.0, 0.0), row_late)
            act.append(row)
            late.append(row_late)
        act8 = [spread(a) > 0.5 for a in act]
        z_on = jnp.where(lane8 < members, mine_f, 0.0) > 0.5
        pick_w = act8 + [z_on, lane8 == 0]
        pick_b = act8 + [z_on, lane8 < 0]

        start = pl.multiple_of(p * obs, obs)
        rows = pl.ds(start, obs)
        wp = [[w_ref[t, pl.ds(pl.multiple_of(start + i * SUBS, SUBS), SUBS), :] for i in range(blocks)]
              for t in range(width)]
        shift = lax.rem(LANES - lax.rem(p, per) * obs, LANES)
        gram = w_ref[lax.div(p, per), rows, :] * inv
        gram = pltpu.roll(gram, shift, 1)
        cols = [[jnp.broadcast_to(gram[i * SUBS:(i + 1) * SUBS, j:j + 1], (SUBS, LANES)) if i >= j // SUBS else None
                 for i in range(blocks)] for j in range(obs)]
        gains, alphas = [], []
        for e in range(blocks):
            gain8 = jnp.zeros((SUBS, LANES), jnp.float32)
            ratio8 = jnp.zeros((SUBS, LANES), jnp.float32)
            scaled = []
            for r in range(SUBS):
                k = e * SUBS + r
                col = cols[k]
                var = var_ref[b, k]
                g = 1.0 / (spread(col[e][r:r + 1, :]) + var)
                gain8 = jnp.where(sub8 == r, g, gain8)
                ratio8 = jnp.where(sub8 == r, var * g, ratio8)
                scale = [None] * e + [col[i] * g for i in range(e, blocks)]
                for i in range(e, blocks):
                    cov_ref[k, i * SUBS:(i + 1) * SUBS, :] = col[i]
                for n in range(k + 1, obs):
                    if n == k + 1:
                        factor = spread(col[n // SUBS][n % SUBS:n % SUBS + 1, :])
                    else:
                        factor = cov_ref[k, pl.ds(n, SUBS, stride=0), :]
                    for i in range(n // SUBS, blocks):
                        cols[n][i] = cols[n][i] - scale[i] * factor
                scale[e] = jnp.where(sub8 > r, scale[e], 0.0)
                scaled.append(scale)
            alpha8 = 1.0 / (1.0 + jnp.sqrt(ratio8))
            gains.append(gain8)
            alphas.append(alpha8)
            for r in range(SUBS):
                alpha = spread(alpha8[r:r + 1, :])
                for t in range(width):
                    u = spread(wp[t][e][r:r + 1, :])
                    both = jnp.where(pick_w[t], u, alpha * u)
                    for i in range(e, blocks):
                        wp[t][i] = wp[t][i] - scaled[r][i] * both
        for i in range(blocks):
            gain = gains[i] * inv
            alpha = alphas[i]
            own = slice(i * SUBS, (i + 1) * SUBS)
            off = slice(obs + i * SUBS, obs + (i + 1) * SUBS)
            for t in range(width):
                here = slice(t * LANES, (t + 1) * LANES)
                reduced = alpha * wp[t][i]
                right_ref[own, here] = jnp.where(pick_w[t], wp[t][i], reduced)
                right_ref[off, here] = jnp.where(pick_b[t], reduced, 0.0)
                if t < tiles:
                    d = wp[t][i] * (late[t] * gain)
                    left_ref[own, here] = d * act[t]
                    left_ref[off, here] = d * (1.0 - act[t])
            at = pl.ds(pl.multiple_of(start + i * SUBS, SUBS), SUBS)
            z_ref[at, :] = wp[tiles][i] * mine_f
            miss = jnp.broadcast_to(wp[width - 1][i][:, :1], (SUBS, LANES))
            v_ref[at, :] = (miss - alpha * wp[tiles][i]) * gain

        for low in range(tiles):
            @pl.when((p < batches - 1) & (lax.div(p + 1, per) == low))
            def _():
                update = contract(left_ref[:, low * LANES:], right_ref[:, low * LANES:])
                for t in range(low, width):
                    w_ref[t, low * LANES:, :] = w_ref[t, low * LANES:, :] - update[:, (t - low) * LANES:(t - low + 1) * LANES]

        return carry

    lax.fori_loop(0, batches, batch, 0)
    moved = contract(v_ref[...], z_ref[...])
    mat = moved[members:members + half, :members]
    out_ref[...] = left_factor(mat)
    mine_ref[...] = left_factor(mat[:, :half])
    theirs_ref[...] = left_factor(mat[:, half:])


def chain(part, back, obs_value, obs_var, owner_tile, tile_mask, batch_order, tile):
    members, total = part.shape[0], 2 * part.shape[1]
    half = members // 2
    obs = obs_value.shape[1]
    width = total // LANES + 2
    f32 = jnp.float32
    return pl.pallas_call(
        chain_kernel,
        out_shape=[pltpu.VMEM((3 * half, 3 * k), jnp.bfloat16) for k in (members, half, half)],
        in_specs=[SMEM] * 5 + [VMEM] * 3,
        out_specs=[VMEM] * 3,
        scratch_shapes=[
            pltpu.VMEM((width, total, LANES), f32),
            pltpu.VMEM((2 * obs, total), f32),
            pltpu.VMEM((2 * obs, width * LANES), f32),
            pltpu.VMEM((total, LANES), f32),
            pltpu.VMEM((total, LANES), f32),
            pltpu.VMEM((obs_value.shape[0], LANES), f32),
            pltpu.VMEM((obs, obs, LANES), f32),
        ],
        compiler_params=pltpu.CompilerParams(vmem_limit_bytes=8 << 20),
        name="chain",
    )(batch_order, owner_tile, tile_mask, obs_var, tile, vmem(part), vmem(back), obs_value)


def times(left, x):
    half = left.shape[0] // 3
    y = jnp.dot(left, jnp.concatenate(thirds(x), axis=0), preferred_element_type=jnp.float32)
    return (y[2 * half:] + y[half:2 * half]) + y[:half]


def apply_block(left, own, upper, lower):
    return own + times(left, jnp.concatenate([own, upper, lower], axis=0))


def apply_main(mat_ref, mine_ref, own_first_ref, own_main_ref, own_last_ref, first_ref, main_ref, out_hbm, part_ref,
               new_ref, sem_out):
    chans = new_ref.shape[0]
    ahead = first_ref.shape[0]
    stores = [pltpu.make_async_copy(new_ref.at[c], out_hbm.at[c], sem_out.at[c]) for c in range(chans)]
    left = mat_ref[...]

    def pair(a, b, c):
        return [a[u] if u < ahead else b[u - ahead] for u in (2 * c, 2 * c + 1)]

    for c in range(chans):
        own = jnp.concatenate(pair(own_first_ref, own_main_ref, c), axis=0)
        new_ref[c] = apply_block(left, own, *pair(first_ref, main_ref, c))
        stores[c].start()
    for c in range(part_ref.shape[0]):
        own = jnp.concatenate([own_last_ref[2 * c], own_last_ref[2 * c + 1]], axis=0)
        part_ref[c] = own + times(mine_ref[...], own)
    for store in stores:
        store.wait()


def apply_last(theirs_ref, part_ref, last_ref, prev_hbm, out_hbm, new_ref, sem_out):
    chans, _, cells = new_ref.shape
    start = out_hbm.shape[0] - chans
    cuts = sem_out.shape[1]
    wide = cells // cuts
    left = theirs_ref[...]
    stores = []
    for c in range(chans):
        for q in range(cuts):
            here = pl.ds(q * wide, wide)
            oth = jnp.concatenate([last_ref[2 * c, :, here], last_ref[2 * c + 1, :, here]], axis=0)
            new_ref[c, :, here] = part_ref[c, :, here] + times(left, oth)
            stores.append(
                pltpu.make_async_copy(new_ref.at[c, :, here], out_hbm.at[start + c, :, here], sem_out.at[c, q]))
            stores[-1].start()
    for store in stores:
        store.wait()


def apply_matrix(mat, mine, theirs, shape, own_first, own_main, own_last, first, main, last):
    chans, half, cells = shape
    tail = last.shape[0] // 2
    head = chans - tail
    f32 = jnp.float32
    state = pltpu.HBM(shape, f32)
    params = pltpu.CompilerParams(vmem_limit_bytes=8 << 20)
    out, part = pl.pallas_call(
        apply_main,
        out_shape=(state, pltpu.VMEM((tail, half, cells), f32)),
        in_specs=[VMEM] * 7,
        out_specs=(ANY, VMEM),
        scratch_shapes=[pltpu.VMEM((head, half, cells), f32), pltpu.SemaphoreType.DMA((head,))],
        compiler_params=params,
        name="apply_main",
    )(vmem(mat), vmem(mine), vmem(own_first), vmem(own_main), vmem(own_last), vmem(first), vmem(main))
    return pl.pallas_call(
        apply_last,
        out_shape=state,
        in_specs=[VMEM, VMEM, VMEM, ANY],
        out_specs=ANY,
        input_output_aliases={3: 0},
        scratch_shapes=[pltpu.VMEM((tail, half, cells), f32), pltpu.SemaphoreType.DMA((tail, 4))],
        compiler_params=params,
        name="apply_last",
    )(vmem(theirs), vmem(part), vmem(last), hbm(out))


def body(ensemble, obs_site, obs_value, obs_var, owner_tile, tile_mask, batch_order):
    tile = lax.axis_index("tile").astype(jnp.int32).reshape(1)
    n_tile = lax.axis_size("tile")
    swap = [(0, 1), (1, 0)]
    ens = jnp.transpose(ensemble, (1, 0, 2))
    chans, half, cells = ens.shape
    units = ens.reshape(2 * chans, half // 2, cells)
    head, tail = 4, 2

    def across(x, step):
        return lax.ppermute(x, "tile", [(i, i ^ step) for i in range(n_tile)])

    own_first = first_units(units, head)
    first = lax.ppermute(own_first, "mem", swap)
    own, own_main, own_last = gather_rows(units, own_first, obs_site, owner_tile, batch_order, tail)
    own = own + across(own, 1)
    cut = own.shape[1] // 2
    own = jnp.where(lax.rem(tile[0], 2) == 0, own[:, :cut], own[:, cut:])
    own = own + across(own, 2)
    low = lax.rem(lax.div(tile[0], 2), 2) == 0
    cut = own.shape[0] // 2
    own = jnp.where(low, own[:cut], own[cut:])
    oth = lax.ppermute(own, "mem", swap)
    main = lax.ppermute(own_main, "mem", swap)
    last = lax.ppermute(own_last, "mem", swap)
    part = jnp.concatenate([own, oth], axis=0)
    step = 4
    while step < n_tile:
        part = part + across(part, step)
        step *= 2
    other = lax.ppermute(part, "tile", [(i, i ^ 2) for i in range(n_tile)])
    upper, lower = jnp.where(low, part, other), jnp.where(low, other, part)
    part = jnp.concatenate([upper[:cut], lower[:cut], upper[cut:], lower[cut:]], axis=0)
    back = lax.ppermute(part, "tile", [(i, i ^ 1) for i in range(n_tile)])
    mat, mine, theirs = chain(part, back, obs_value, obs_var, owner_tile, tile_mask, batch_order, tile)
    out = apply_matrix(mat, mine, theirs, ens.shape, own_first, own_main, own_last, first, main, last)
    return jnp.transpose(out, (1, 0, 2))


def solution(mesh):
    return jax.shard_map(
        body,
        mesh=mesh,
        in_specs=(P("mem", None, "tile"), P(), P(), P(), P(), P(), P()),
        out_specs=P("mem", None, "tile"),
        check_vma=False,
    )
```

```python
import functools

import jax
import jax.numpy as jnp
from jax import lax
from jax.experimental import pallas as pl
from jax.experimental.pallas import tpu as pltpu
from jax.sharding import PartitionSpec as P


LANES = 128
SUBS = 8
SMEM = pl.BlockSpec(memory_space=pltpu.SMEM)
VMEM = pl.BlockSpec(memory_space=pltpu.VMEM)
ANY = pl.BlockSpec(memory_space=pl.ANY)


def hbm(x):
    return pltpu.with_memory_space_constraint(x, pltpu.HBM)


def vmem(x):
    return pltpu.with_memory_space_constraint(x, pltpu.VMEM)


def first_kernel(units_hbm, first_ref, sem):
    copy = pltpu.make_async_copy(units_hbm.at[pl.ds(0, first_ref.shape[0])], first_ref, sem)
    copy.start()
    copy.wait()


def first_units(units, count):
    return pl.pallas_call(
        first_kernel,
        out_shape=pltpu.VMEM((count,) + units.shape[1:], jnp.float32),
        in_specs=[ANY],
        out_specs=VMEM,
        scratch_shapes=[pltpu.SemaphoreType.DMA],
        name="first_units",
    )(hbm(units))


def split(value, size):
    if size & (size - 1) == 0:
        return lax.shift_right_logical(value, size.bit_length() - 1), lax.bitwise_and(value, size - 1)
    quotient = lax.div(value, size)
    return quotient, value - quotient * size


def gather_kernel(site_hbm, owner_hbm, order_hbm, units_hbm, first_ref, rows_ref, main_ref, last_ref,
                  site_ref, owner_ref, order_ref, sem):
    batches, obs = site_hbm.shape
    count, half, cells = units_hbm.shape
    per = LANES // obs
    head, middle, tail = first_ref.shape[0], main_ref.shape[0], last_ref.shape[0]
    copies = [
        pltpu.make_async_copy(owner_hbm, owner_ref, sem.at[0]),
        pltpu.make_async_copy(order_hbm, order_ref, sem.at[1]),
        pltpu.make_async_copy(site_hbm, site_ref, sem.at[2]),
        pltpu.make_async_copy(units_hbm.at[pl.ds(head, middle)], main_ref, sem.at[3]),
        pltpu.make_async_copy(units_hbm.at[pl.ds(count - tail, tail)], last_ref, sem.at[4]),
    ]
    for copy in copies:
        copy.start()
    tile = lax.axis_index("tile")
    lane = lax.broadcasted_iota(jnp.int32, (half, LANES), 1)
    rows_ref[...] = jnp.zeros_like(rows_ref)
    for copy in copies:
        copy.wait()

    def one(p, carry):
        b = order_ref[p]

        @pl.when(owner_ref[b] == tile)
        def _():
            group, place = split(p, per)
            base = place * obs
            spot = pl.ds(pl.multiple_of(group * LANES, LANES), LANES)
            acc = [rows_ref[h * half:(h + 1) * half, spot] for h in range(2)]
            for k in range(obs):
                chan, cell = split(site_ref[b, k], cells)
                _, col = split(cell, LANES)
                here = pl.ds(pl.multiple_of(cell - col, LANES), LANES)
                at = base + k
                turn = lax.bitwise_and(at - col, LANES - 1)
                mine = lane == at
                for h in range(2):
                    unit = 2 * chan + h
                    block = main_ref[jnp.clip(unit - head, 0, middle - 1), :, here]
                    early = first_ref[jnp.minimum(unit, head - 1), :, here]
                    late = last_ref[jnp.clip(unit - (count - tail), 0, tail - 1), :, here]
                    block = jnp.where(unit < head, early, jnp.where(unit >= count - tail, late, block))
                    acc[h] = jnp.where(mine, pltpu.roll(block, turn, 1), acc[h])
            for h in range(2):
                rows_ref[h * half:(h + 1) * half, spot] = acc[h]

        return carry

    lax.fori_loop(0, batches, one, 0)


def gather_rows(units, first, obs_site, owner_tile, batch_order, tail):
    batches, obs = obs_site.shape
    count, half, cells = units.shape
    f32 = jnp.float32
    return pl.pallas_call(
        gather_kernel,
        out_shape=(
            pltpu.VMEM((2 * half, batches * obs), f32),
            pltpu.VMEM((count - first.shape[0] - tail, half, cells), f32),
            pltpu.VMEM((tail, half, cells), f32),
        ),
        in_specs=[ANY] * 4 + [VMEM],
        out_specs=(VMEM, VMEM, VMEM),
        scratch_shapes=[
            pltpu.SMEM(obs_site.shape, jnp.int32),
            pltpu.SMEM(owner_tile.shape, jnp.int32),
            pltpu.SMEM(batch_order.shape, jnp.int32),
            pltpu.SemaphoreType.DMA((5,)),
        ],
        compiler_params=pltpu.CompilerParams(vmem_limit_bytes=8 << 20),
        name="gather_rows",
    )(hbm(obs_site), hbm(owner_tile), hbm(batch_order), hbm(units), vmem(first))


def spread(row):
    return jnp.broadcast_to(row, (SUBS, row.shape[1]))


def thirds(x):
    parts = []
    for _ in range(3):
        parts.append(x.astype(jnp.bfloat16))
        x = x - parts[-1].astype(jnp.float32)
    return parts


def left_factor(mat):
    high, mid, low = thirds(mat)
    zero = jnp.zeros_like(low)
    return jnp.concatenate([
        jnp.concatenate([high, high, high], axis=1),
        jnp.concatenate([mid, mid, zero], axis=1),
        jnp.concatenate([low, zero, zero], axis=1),
    ], axis=0)


def chain_kernel(order_ref, owner_ref, mask_ref, var_ref, tile_ref, part_ref, back_ref, val_ref,
                 out_ref, mine_ref, theirs_ref, w_ref, left_ref, right_ref, z_ref, v_ref, val_s, cov_ref):
    batches, obs = val_ref.shape
    members = part_ref.shape[0]
    half = members // 2
    total = batches * obs
    tiles = total // LANES
    per = LANES // obs
    blocks = obs // SUBS
    width = w_ref.shape[0]
    inv = 1.0 / (members - 1)
    highest = lax.Precision.HIGHEST
    contract = functools.partial(
        lax.dot_general, dimension_numbers=(((0,), (0,)), ((), ())), precision=highest,
        preferred_element_type=jnp.float32)
    lane1 = lax.broadcasted_iota(jnp.int32, (1, LANES), 1)
    lane8 = lax.broadcasted_iota(jnp.int32, (SUBS, LANES), 1)
    sub8 = lax.broadcasted_iota(jnp.int32, (SUBS, LANES), 0)
    tile = tile_ref[0]

    val_s[...] = jnp.zeros_like(val_s)
    val_s[:, :obs] = val_ref[...]
    values = []
    for t in range(tiles):
        row = jnp.zeros((1, LANES), jnp.float32)
        for q in range(per):
            one = val_s[pl.ds(order_ref[t * per + q], 1), :]
            row = row + (pltpu.roll(one, q * obs, 1) if q else one)
        values.append(row)
    values = jnp.concatenate(values, axis=1)

    part, back = part_ref[...], back_ref[...]
    even = lax.rem(tile, 2) == 0
    raw = jnp.concatenate([jnp.where(even, part, back), jnp.where(even, back, part)], axis=1)
    mean = jnp.sum(raw, axis=0, keepdims=True) * (1.0 / members)
    anom = raw - mean
    first = lax.broadcasted_iota(jnp.int32, (SUBS, total), 0) == 0
    lhs = jnp.concatenate([anom, jnp.where(first, values - mean, 0.0)], axis=0)
    depth = members + SUBS
    r_i = lax.broadcasted_iota(jnp.int32, (depth, 2 * LANES), 0)
    l_i = lax.broadcasted_iota(jnp.int32, (depth, 2 * LANES), 1)
    pick = jnp.where((r_i < members) & ((l_i == r_i) | (l_i == r_i + members)), 1.0, 0.0)
    pick = jnp.where((r_i == members) & (l_i == LANES), 1.0, pick)
    rhs = jnp.concatenate(
        [jnp.concatenate([anom, jnp.zeros((SUBS, total), jnp.float32)], axis=0), pick], axis=1)
    full = contract(lhs, rhs)
    for t in range(width):
        w_ref[t] = full[:, t * LANES:(t + 1) * LANES]

    def batch(p, carry):
        b = order_ref[p]
        o = owner_ref[b]
        mine = (mask_ref[b, tile] == 1) | (o == tile)
        mine_f = jnp.where(mine, 1.0, 0.0)
        act = []
        late = []
        for t in range(tiles):
            row = jnp.zeros((1, LANES), jnp.float32)
            row_late = jnp.zeros((1, LANES), jnp.float32)
            for q in range(per):
                other = owner_ref[order_ref[t * per + q]]
                on = (mask_ref[b, other] == 1) | (o == other)
                here = (lane1 >= q * obs) & (lane1 < (q + 1) * obs)
                row = jnp.where(here, jnp.where(on, 1.0, 0.0), row)
                row_late = jnp.where(here, jnp.where(t * per + q > p, 1.0, 0.0), row_late)
            act.append(row)
            late.append(row_late)
        act8 = [spread(a) > 0.5 for a in act]
        z_on = jnp.where(lane8 < members, mine_f, 0.0) > 0.5
        pick_w = act8 + [z_on, lane8 == 0]
        pick_b = act8 + [z_on, lane8 < 0]

        start = pl.multiple_of(p * obs, obs)
        rows = pl.ds(start, obs)
        wp = [[w_ref[t, pl.ds(pl.multiple_of(start + i * SUBS, SUBS), SUBS), :] for i in range(blocks)]
              for t in range(width)]
        shift = lax.rem(LANES - lax.rem(p, per) * obs, LANES)
        gram = w_ref[lax.div(p, per), rows, :] * inv
        gram = pltpu.roll(gram, shift, 1)
        cols = [[jnp.broadcast_to(gram[i * SUBS:(i + 1) * SUBS, j:j + 1], (SUBS, LANES)) if i >= j // SUBS else None
                 for i in range(blocks)] for j in range(obs)]
        gains, alphas = [], []
        for e in range(blocks):
            gain8 = jnp.zeros((SUBS, LANES), jnp.float32)
            ratio8 = jnp.zeros((SUBS, LANES), jnp.float32)
            scaled = []
            for r in range(SUBS):
                k = e * SUBS + r
                col = cols[k]
                var = var_ref[b, k]
                g = 1.0 / (spread(col[e][r:r + 1, :]) + var)
                gain8 = jnp.where(sub8 == r, g, gain8)
                ratio8 = jnp.where(sub8 == r, var * g, ratio8)
                scale = [None] * e + [col[i] * g for i in range(e, blocks)]
                for i in range(e, blocks):
                    cov_ref[k, i * SUBS:(i + 1) * SUBS, :] = col[i]
                for n in range(k + 1, obs):
                    if n == k + 1:
                        factor = spread(col[n // SUBS][n % SUBS:n % SUBS + 1, :])
                    else:
                        factor = cov_ref[k, pl.ds(n, SUBS, stride=0), :]
                    for i in range(n // SUBS, blocks):
                        cols[n][i] = cols[n][i] - scale[i] * factor
                scale[e] = jnp.where(sub8 > r, scale[e], 0.0)
                scaled.append(scale)
            alpha8 = 1.0 / (1.0 + jnp.sqrt(ratio8))
            gains.append(gain8)
            alphas.append(alpha8)
            for r in range(SUBS):
                alpha = spread(alpha8[r:r + 1, :])
                for t in range(width):
                    u = spread(wp[t][e][r:r + 1, :])
                    both = jnp.where(pick_w[t], u, alpha * u)
                    for i in range(e, blocks):
                        wp[t][i] = wp[t][i] - scaled[r][i] * both
        for i in range(blocks):
            gain = gains[i] * inv
            alpha = alphas[i]
            own = slice(i * SUBS, (i + 1) * SUBS)
            off = slice(obs + i * SUBS, obs + (i + 1) * SUBS)
            for t in range(width):
                here = slice(t * LANES, (t + 1) * LANES)
                reduced = alpha * wp[t][i]
                right_ref[own, here] = jnp.where(pick_w[t], wp[t][i], reduced)
                right_ref[off, here] = jnp.where(pick_b[t], reduced, 0.0)
                if t < tiles:
                    d = wp[t][i] * (late[t] * gain)
                    left_ref[own, here] = d * act[t]
                    left_ref[off, here] = d * (1.0 - act[t])
            at = pl.ds(pl.multiple_of(start + i * SUBS, SUBS), SUBS)
            z_ref[at, :] = wp[tiles][i] * mine_f
            miss = jnp.broadcast_to(wp[width - 1][i][:, :1], (SUBS, LANES))
            v_ref[at, :] = (miss - alpha * wp[tiles][i]) * gain

        for low in range(tiles):
            @pl.when((p < batches - 1) & (lax.div(p + 1, per) == low))
            def _():
                update = contract(left_ref[:, low * LANES:], right_ref[:, low * LANES:])
                for t in range(low, width):
                    w_ref[t, low * LANES:, :] = w_ref[t, low * LANES:, :] - update[:, (t - low) * LANES:(t - low + 1) * LANES]

        return carry

    lax.fori_loop(0, batches, batch, 0)
    moved = contract(v_ref[...], z_ref[...])
    mat = moved[members:members + half, :members]
    out_ref[...] = left_factor(mat)
    mine_ref[...] = left_factor(mat[:, :half])
    theirs_ref[...] = left_factor(mat[:, half:])


def chain(part, back, obs_value, obs_var, owner_tile, tile_mask, batch_order, tile):
    members, total = part.shape[0], 2 * part.shape[1]
    half = members // 2
    obs = obs_value.shape[1]
    width = total // LANES + 2
    f32 = jnp.float32
    return pl.pallas_call(
        chain_kernel,
        out_shape=[pltpu.VMEM((3 * half, 3 * k), jnp.bfloat16) for k in (members, half, half)],
        in_specs=[SMEM] * 5 + [VMEM] * 3,
        out_specs=[VMEM] * 3,
        scratch_shapes=[
            pltpu.VMEM((width, total, LANES), f32),
            pltpu.VMEM((2 * obs, total), f32),
            pltpu.VMEM((2 * obs, width * LANES), f32),
            pltpu.VMEM((total, LANES), f32),
            pltpu.VMEM((total, LANES), f32),
            pltpu.VMEM((obs_value.shape[0], LANES), f32),
            pltpu.VMEM((obs, obs, LANES), f32),
        ],
        compiler_params=pltpu.CompilerParams(vmem_limit_bytes=8 << 20),
        name="chain",
    )(batch_order, owner_tile, tile_mask, obs_var, tile, vmem(part), vmem(back), obs_value)


def times(left, x):
    half = left.shape[0] // 3
    y = jnp.dot(left, jnp.concatenate(thirds(x), axis=0), preferred_element_type=jnp.float32)
    return (y[2 * half:] + y[half:2 * half]) + y[:half]


def apply_block(left, own, upper, lower):
    return own + times(left, jnp.concatenate([own, upper, lower], axis=0))


def apply_main(mat_ref, mine_ref, own_first_ref, own_main_ref, own_last_ref, first_ref, main_ref, out_hbm, part_ref,
               new_ref, sem_out):
    chans = new_ref.shape[0]
    ahead = first_ref.shape[0]
    stores = [pltpu.make_async_copy(new_ref.at[c], out_hbm.at[c], sem_out.at[c]) for c in range(chans)]
    left = mat_ref[...]

    def pair(a, b, c):
        return [a[u] if u < ahead else b[u - ahead] for u in (2 * c, 2 * c + 1)]

    for c in range(chans):
        own = jnp.concatenate(pair(own_first_ref, own_main_ref, c), axis=0)
        new_ref[c] = apply_block(left, own, *pair(first_ref, main_ref, c))
        stores[c].start()
    for c in range(part_ref.shape[0]):
        own = jnp.concatenate([own_last_ref[2 * c], own_last_ref[2 * c + 1]], axis=0)
        part_ref[c] = own + times(mine_ref[...], own)
    for store in stores:
        store.wait()


def apply_last(theirs_ref, part_ref, last_ref, prev_hbm, out_hbm, new_ref, sem_out):
    chans, _, cells = new_ref.shape
    start = out_hbm.shape[0] - chans
    cuts = sem_out.shape[1]
    wide = cells // cuts
    left = theirs_ref[...]
    stores = []
    for c in range(chans):
        for q in range(cuts):
            here = pl.ds(q * wide, wide)
            oth = jnp.concatenate([last_ref[2 * c, :, here], last_ref[2 * c + 1, :, here]], axis=0)
            new_ref[c, :, here] = part_ref[c, :, here] + times(left, oth)
            stores.append(
                pltpu.make_async_copy(new_ref.at[c, :, here], out_hbm.at[start + c, :, here], sem_out.at[c, q]))
            stores[-1].start()
    for store in stores:
        store.wait()


def apply_matrix(mat, mine, theirs, shape, own_first, own_main, own_last, first, main, last):
    chans, half, cells = shape
    tail = last.shape[0] // 2
    head = chans - tail
    f32 = jnp.float32
    state = pltpu.HBM(shape, f32)
    params = pltpu.CompilerParams(vmem_limit_bytes=8 << 20)
    out, part = pl.pallas_call(
        apply_main,
        out_shape=(state, pltpu.VMEM((tail, half, cells), f32)),
        in_specs=[VMEM] * 7,
        out_specs=(ANY, VMEM),
        scratch_shapes=[pltpu.VMEM((head, half, cells), f32), pltpu.SemaphoreType.DMA((head,))],
        compiler_params=params,
        name="apply_main",
    )(vmem(mat), vmem(mine), vmem(own_first), vmem(own_main), vmem(own_last), vmem(first), vmem(main))
    return pl.pallas_call(
        apply_last,
        out_shape=state,
        in_specs=[VMEM, VMEM, VMEM, ANY],
        out_specs=ANY,
        input_output_aliases={3: 0},
        scratch_shapes=[pltpu.VMEM((tail, half, cells), f32), pltpu.SemaphoreType.DMA((tail, 2))],
        compiler_params=params,
        name="apply_last",
    )(vmem(theirs), vmem(part), vmem(last), hbm(out))


def body(ensemble, obs_site, obs_value, obs_var, owner_tile, tile_mask, batch_order):
    tile = lax.axis_index("tile").astype(jnp.int32).reshape(1)
    n_tile = lax.axis_size("tile")
    swap = [(0, 1), (1, 0)]
    ens = jnp.transpose(ensemble, (1, 0, 2))
    chans, half, cells = ens.shape
    units = ens.reshape(2 * chans, half // 2, cells)
    head, tail = 3, 2

    def across(x, step):
        return lax.ppermute(x, "tile", [(i, i ^ step) for i in range(n_tile)])

    own_first = first_units(units, head)
    first = lax.ppermute(own_first, "mem", swap)
    own, own_main, own_last = gather_rows(units, own_first, obs_site, owner_tile, batch_order, tail)
    own = own + across(own, 1)
    cut = own.shape[1] // 2
    own = jnp.where(lax.rem(tile[0], 2) == 0, own[:, :cut], own[:, cut:])
    oth = lax.ppermute(own, "mem", swap)
    main = lax.ppermute(own_main, "mem", swap)
    last = lax.ppermute(own_last, "mem", swap)
    part = jnp.concatenate([own, oth], axis=0)
    step = 2
    while step < n_tile:
        part = part + across(part, step)
        step *= 2
    back = lax.ppermute(part, "tile", [(i, i ^ 1) for i in range(n_tile)])
    mat, mine, theirs = chain(part, back, obs_value, obs_var, owner_tile, tile_mask, batch_order, tile)
    out = apply_matrix(mat, mine, theirs, ens.shape, own_first, own_main, own_last, first, main, last)
    return jnp.transpose(out, (1, 0, 2))


def solution(mesh):
    return jax.shard_map(
        body,
        mesh=mesh,
        in_specs=(P("mem", None, "tile"), P(), P(), P(), P(), P(), P()),
        out_specs=P("mem", None, "tile"),
        check_vma=False,
    )
```
